32 devices in a mesh: ctx: 8 (over z, x), head: 4 (over y, core).
Axes of the slice: x: 2, y: 2, z: 4, core: 2. Of those that a mesh axis runs over, the one named last changes fastest.
Arguments:
- video_rows: bfloat16 [4096, 5120], P('ctx'), may hold values from -6 to 6
- w_query: bfloat16 [5120, 5120], P('ctx', 'head'), may hold values from -0.078125 to 0.078125
- w_output: bfloat16 [5120, 5120], P('ctx', 'head'), may hold values from -0.078125 to 0.078125
- audio_tokens: bfloat16 [2, 32, 768], P(None, 'ctx'), may hold values from -544 to 544
- w_key: bfloat16 [768, 5120], P(None, 'head'), may hold values from -0.21875 to 0.21875
- w_value: bfloat16 [768, 5120], P(None, 'head'), may hold values from -0.21875 to 0.21875
- row_lists: int32 [2, 4096], P(None, 'ctx'), may hold values from 0 to 511, as said below
- row_counts: int32 [2, 8], P(None, 'ctx'), may hold values from 0 to 512, as said below
Outputs:
- layer_out: bfloat16 [4096, 5120], P('ctx', 'head')
The draws below stay inside these ranges and needn't reach their ends.
Inputs may be any that keep to these rules, and one draw needn't show every extreme that they name: `row_lists`: the first row_counts[s, c] entries of speaker s's block on shard c are distinct, live entries of the two speakers on one shard are distinct rows, and the other entries are arbitrary row numbers of the shard. `row_counts`: on each shard the two counts add up to at most 512.
All inputs are finite; a program needn't handle non-finite values.
Results may differ from the reference program's by a relative error of at most 0.0045.
The reference program's roundings to bfloat16 on the way count: a program that leaves them out, or rounds other values in their place, can miss the bound.
Values may be sent and summed in bfloat16 or wider, within the bound.
No kernel may reach another device: no remote copies, remote signals or barrier semaphores. Data moves between devices by JAX's collectives and lax.ppermute only.
A program may use at most 128 MiB of HBM per device.

```python
import jax
import jax.numpy as jnp
from jax import lax

D = 5120
HEADS = 40
HD = 128
AW = 768
SPK = 2
ROWS_DEV = 512
SHARDS = 8
ROWS = 4096
AUD = 32


def speaker_layout(key):
    base = jax.random.fold_in(key, 7)
    keys_all = jax.random.split(base, 6)
    shard_ids = jnp.arange(SHARDS, dtype=jnp.int32)
    totals = jax.random.randint(keys_all[0], (SHARDS,), ROWS_DEV // 2, ROWS_DEV + 1)
    firsts = jax.random.randint(keys_all[1], (SHARDS,), 0, totals + 1)
    full_shard = jax.random.randint(keys_all[2], (), 0, SHARDS)
    full_speaker = jax.random.randint(keys_all[3], (), 0, 2)
    count_zero = jnp.where(shard_ids == full_shard, jnp.where(full_speaker == 0, ROWS_DEV, 0), firsts)
    count_one = jnp.where(shard_ids == full_shard, ROWS_DEV - count_zero, totals - firsts)
    counts = jnp.stack([count_zero, count_one]).astype(jnp.int32)
    perm_keys = jax.random.split(keys_all[4], SHARDS)
    orders = jax.vmap(lambda one_key: jax.random.permutation(one_key, ROWS_DEV))(perm_keys).astype(jnp.int32)
    padding = jax.random.randint(keys_all[5], (2, SHARDS, ROWS_DEV), 0, ROWS_DEV)
    slots = jnp.arange(ROWS_DEV, dtype=jnp.int32)[None, :]
    list_zero = jnp.where(slots < count_zero[:, None], orders, padding[0])
    shifted = jnp.clip(count_zero[:, None] + slots, 0, ROWS_DEV - 1)
    second = jnp.take_along_axis(orders, shifted, axis=1)
    list_one = jnp.where(slots < count_one[:, None], second, padding[1])
    lists = jnp.stack([list_zero, list_one]).reshape(2, SHARDS * ROWS_DEV).astype(jnp.int32)
    return (lists, counts)


def draw_row_lists(key, part):
    lists, counts = speaker_layout(key)
    return lists


def draw_row_counts(key, part):
    lists, counts = speaker_layout(key)
    return counts


def draw_audio_tokens(key, part):
    values = jax.random.normal(jax.random.fold_in(key, 4), (SPK, AUD, AW), jnp.float32)
    return jnp.clip(values, -6.0, 6.0).astype(jnp.bfloat16)


def block_levels(key, shape, pieces, least, high):
    loudness, own = 1.0, jax.random.fold_in(key, 6)
    for dim, shards_of in pieces:
        heights = jnp.exp(jax.random.uniform(jax.random.fold_in(own, dim), (shards_of,), jnp.float32, least / len(pieces), high / len(pieces)))
        loudness = loudness * jnp.repeat(heights, shape[dim] // shards_of).reshape([-1 if axis == dim else 1 for axis in range(len(shape))])
    return loudness


def centred(own_key, shape, deviation, most, cuts=(), held_as=jnp.bfloat16):
    values = jax.random.normal(own_key, shape, jnp.float32) * deviation
    if len(cuts) > 0:
        values = block_levels(own_key, shape, cuts, -0.22, 0.18) * values
    return jnp.clip(values, min=-most, max=most).astype(held_as)


def setup_inputs(seed: int = 0) -> dict:
    splits = jax.random.split(jax.random.key(seed), 9)
    video_rows = centred(splits[0], (ROWS, D), 1.0, 6.0, ((0, 8),))
    w_query = centred(splits[1], (D, D), D ** -0.5, 0.078125, ((0, 8), (1, 4)))
    w_output = centred(splits[2], (D, D), D ** -0.5, 0.078125, ((0, 8), (1, 4)))
    audio_tokens = draw_audio_tokens(jax.random.fold_in(splits[8], 71), 0)
    w_key = centred(splits[4], (AW, D), AW ** -0.5, 0.21875, ((1, 4),))
    w_value = centred(splits[5], (AW, D), AW ** -0.5, 0.21875, ((1, 4),))
    row_lists = draw_row_lists(jax.random.fold_in(splits[8], 71), 0)
    row_counts = draw_row_counts(jax.random.fold_in(splits[8], 71), 0)
    return {"video_rows": video_rows, "w_query": w_query, "w_output": w_output, "audio_tokens": audio_tokens, "w_key": w_key, "w_value": w_value, "row_lists": row_lists, "row_counts": row_counts}


def attend(blocks):
    query_head, key_head, value_head = blocks
    scores = jnp.dot(query_head, key_head.T, preferred_element_type=jnp.float32) * (1.0 / (HD ** 0.5))
    scores = scores - jnp.max(scores, axis=-1, keepdims=True)
    weights = jnp.exp(scores)
    weights = (weights / jnp.sum(weights, axis=-1, keepdims=True)).astype(jnp.bfloat16)
    return jnp.dot(weights, value_head, preferred_element_type=jnp.float32).astype(jnp.bfloat16)


def reference(video_rows, w_query, w_output, audio_tokens, w_key, w_value, row_lists, row_counts):
    queries = jnp.dot(video_rows, w_query, preferred_element_type=jnp.float32).astype(jnp.bfloat16)
    audio_flat = audio_tokens.reshape(SPK * AUD, AW)
    key_rows = jnp.dot(audio_flat, w_key, preferred_element_type=jnp.float32).astype(jnp.bfloat16)
    value_rows = jnp.dot(audio_flat, w_value, preferred_element_type=jnp.float32).astype(jnp.bfloat16)
    key_rows = key_rows.reshape(SPK, AUD, HEADS, HD)
    value_rows = value_rows.reshape(SPK, AUD, HEADS, HD)
    position = jnp.arange(ROWS, dtype=jnp.int32)
    shard_of = position // ROWS_DEV
    local_row = position % ROWS_DEV
    summed = jnp.zeros((ROWS, D), jnp.float32)
    for speaker in range(SPK):
        target = (row_lists[speaker] + shard_of * ROWS_DEV).astype(jnp.int32)
        row_live = local_row < row_counts[speaker][shard_of]
        picked = queries[target].reshape(ROWS, HEADS, HD).transpose(1, 0, 2)
        key_block = key_rows[speaker].transpose(1, 0, 2)
        value_block = value_rows[speaker].transpose(1, 0, 2)
        blended = lax.map(attend, (picked, key_block, value_block))
        blended = blended.transpose(1, 0, 2).reshape(ROWS, D).astype(jnp.float32)
        blended = jnp.where(row_live[:, None], blended, jnp.zeros_like(blended))
        summed = summed.at[target].add(blended)
    attended = summed.astype(jnp.bfloat16)
    return jnp.dot(attended, w_output, preferred_element_type=jnp.float32).astype(jnp.bfloat16)
```

```python
import functools

import jax
import jax.numpy as jnp
from jax import lax
from jax.experimental import pallas as pl
from jax.experimental.pallas import tpu as pltpu
from jax.sharding import PartitionSpec as P

HD = 128
SPK = 2
AXES = ("ctx", "head")
QUERY_CHUNKS = (3, 2)
OUT_CHUNKS = (3, 3, 2, 2)


def add_rows(left_rows, shard_piece):
    return jnp.dot(left_rows, shard_piece, preferred_element_type=jnp.float32)


def plain_shards(video_rows, w_query, w_output, audio_tokens, w_key, w_value, row_lists, row_counts):
    rows_dev = video_rows.shape[0]
    columns = w_query.shape[1]
    heads_dev = columns // HD
    queries = add_rows(video_rows, lax.all_gather(w_query, "ctx", axis=0, tiled=True)).astype(
        jnp.bfloat16
    )
    whole_audio = lax.all_gather(audio_tokens, "ctx", axis=1, tiled=True)
    key_rows = jnp.einsum(
        "sta,ad->std", whole_audio, w_key, preferred_element_type=jnp.float32
    ).astype(jnp.bfloat16)
    value_rows = jnp.einsum(
        "sta,ad->std", whole_audio, w_value, preferred_element_type=jnp.float32
    ).astype(jnp.bfloat16)
    audio_length = key_rows.shape[1]
    position = jnp.arange(rows_dev, dtype=jnp.int32)
    score_scale = 1.0 / HD**0.5
    summed = jnp.zeros((rows_dev, columns), jnp.float32)
    for speaker in range(SPK):
        target = row_lists[speaker]
        row_live = position < row_counts[speaker, 0]
        picked = queries[target].reshape(rows_dev, heads_dev, HD)
        key_block = key_rows[speaker].reshape(audio_length, heads_dev, HD)
        value_block = value_rows[speaker].reshape(audio_length, heads_dev, HD)
        scores = (
            jnp.einsum("rhd,khd->hrk", picked, key_block, preferred_element_type=jnp.float32)
            * score_scale
        )
        scores = scores - jnp.max(scores, axis=-1, keepdims=True)
        weights = jnp.exp(scores)
        weights = (weights / jnp.sum(weights, axis=-1, keepdims=True)).astype(jnp.bfloat16)
        blended = jnp.einsum(
            "hrk,khd->rhd", weights, value_block, preferred_element_type=jnp.float32
        ).astype(jnp.bfloat16)
        blended = blended.reshape(rows_dev, columns).astype(jnp.float32)
        blended = jnp.where(row_live[:, None], blended, jnp.zeros_like(blended))
        summed = summed.at[target].add(blended)
    attended = summed.astype(jnp.bfloat16)
    all_heads = lax.all_gather(attended, "head", axis=1, tiled=True)
    result = add_rows(all_heads, lax.all_gather(w_output, "ctx", axis=0, tiled=True))
    return result.astype(jnp.bfloat16)


def pairs(move):
    found = []
    for z in range(4):
        for x in range(2):
            for h in range(4):
                to = move(z, x, h)
                if to is not None:
                    found.append(((2 * z + x) * 4 + h, (2 * to[0] + to[1]) * 4 + to[2]))
    return found


ACROSS_X = pairs(lambda z, x, h: (z, 1 - x, h))
ACROSS_Y = pairs(lambda z, x, h: (z, x, h ^ 2))
ACROSS_CORE = pairs(lambda z, x, h: (z, x, h ^ 1))
SWAP_END = pairs(lambda z, x, h: (z ^ 1, x, h))
END_TO_MID = pairs(lambda z, x, h: (z ^ 1, x, h) if z in (0, 3) else None)
MID_TO_END = pairs(lambda z, x, h: (z ^ 1, x, h) if z in (1, 2) else None)
MID_TO_MID = pairs(lambda z, x, h: (3 - z, x, h) if z in (1, 2) else None)


def send(value, move):
    return lax.ppermute(value, AXES, move)


def product_body(place, *refs, k_sizes):
    *lefts, weights, kept, sent = refs
    total = None
    for j in range(4):
        first = 0
        for i, size in enumerate(k_sizes):
            left = lefts[i * 4 + j][...]
            right = weights[place[j], first : first + size, :]
            term = jnp.dot(left, right, preferred_element_type=jnp.float32)
            total = term if total is None else total + term
            first += size
    half = kept.shape[1]
    kept[...] = total[:, :half]
    sent[...] = total[:, half:]


def query_product(place, lefts, weights, rows, from_columns):
    depth, columns = weights.shape[1:]
    step = min(rows, 512)
    if from_columns:
        left_specs = [
            pl.BlockSpec((step, depth), functools.partial(lambda j, i, place: (i, place[4 + j]), j))
            for j in range(4)
        ]
    else:
        left_specs = [pl.BlockSpec((step, depth), lambda i, place: (i, 0)) for _ in range(4)]
    half = columns // 2
    part = jax.ShapeDtypeStruct((rows, half), jnp.float32)
    return pl.pallas_call(
        functools.partial(product_body, k_sizes=(depth,)),
        grid_spec=pltpu.PrefetchScalarGridSpec(
            num_scalar_prefetch=1,
            grid=(rows // step,),
            in_specs=left_specs + [pl.BlockSpec(weights.shape, lambda i, place: (0, 0, 0))],
            out_specs=[pl.BlockSpec((step, half), lambda i, place: (i, 0))] * 2,
        ),
        out_shape=[part, part],
        name="query_product",
    )(place, *lefts, weights)


def out_body(place, *refs, k_sizes):
    *lefts, weights, total_out = refs
    total = None
    for j in range(4):
        first = 0
        for i, size in enumerate(k_sizes):
            left = lefts[i * 4 + j][...]
            right = weights[place[j], first : first + size, :]
            term = jnp.dot(left, right, preferred_element_type=jnp.float32)
            total = term if total is None else total + term
            first += size
    total_out[...] = total


def out_product(place, lefts, weights, k_sizes):
    rows = lefts[0].shape[0]
    columns = weights.shape[2]
    step = rows // 2
    left_specs = [
        pl.BlockSpec((step, size), lambda i, place: (i, 0)) for size in k_sizes for _ in range(4)
    ]
    return pl.pallas_call(
        functools.partial(out_body, k_sizes=k_sizes),
        grid_spec=pltpu.PrefetchScalarGridSpec(
            num_scalar_prefetch=1,
            grid=(2,),
            in_specs=left_specs + [pl.BlockSpec(weights.shape, lambda i, place: (0, 0, 0))],
            out_specs=pl.BlockSpec((step, columns), lambda i, place: (i, 0)),
        ),
        out_shape=jax.ShapeDtypeStruct((rows, columns), jnp.float32),
        name="out_product",
    )(place, *lefts, weights)


def attend_body(kept, received, keys, values, speaker, attended, *, audio_length, heads):
    scale = 1.0 / HD**0.5
    of_row = speaker[...]
    lane = lax.broadcasted_iota(jnp.int32, (kept.shape[0], SPK * audio_length), 1)
    of_key = jnp.where(lane < audio_length, 1, 2)
    own_key = of_key == of_row
    live = of_row > 0
    for head in range(heads):
        at = slice(head * HD, (head + 1) * HD)
        query = (kept[:, at] + received[:, at]).astype(jnp.bfloat16)
        scores = (
            lax.dot_general(
                query, keys[:, at], (((1,), (1,)), ((), ())), preferred_element_type=jnp.float32
            )
            * scale
        )
        scores = jnp.where(own_key, scores, -1e30)
        scores = scores - jnp.max(scores, axis=-1, keepdims=True)
        weights = jnp.exp(scores)
        weights = (weights / jnp.sum(weights, axis=-1, keepdims=True)).astype(jnp.bfloat16)
        blended = jnp.dot(weights, values[:, at], preferred_element_type=jnp.float32)
        attended[:, at] = jnp.where(live, blended, 0.0).astype(jnp.bfloat16)


def attend(kept, received, keys, values, speaker, audio_length, swap):
    rows, columns = kept.shape
    step = rows // 2 if swap else min(rows, 512)
    count = rows // step
    flip = (lambda i: (count - 1 - i, 0)) if swap else (lambda i: (i, 0))
    at = lambda i: (i, 0)
    whole = pl.BlockSpec(keys.shape, lambda i: (0, 0))
    return pl.pallas_call(
        functools.partial(attend_body, audio_length=audio_length, heads=columns // HD),
        grid=(count,),
        in_specs=[
            pl.BlockSpec((step, columns), at),
            pl.BlockSpec((step, columns), flip),
            whole,
            whole,
            pl.BlockSpec((step, 1), at),
        ],
        out_specs=pl.BlockSpec((step, columns), at),
        out_shape=jax.ShapeDtypeStruct((rows, columns), jnp.bfloat16),
        name="attend",
    )(kept, received, keys, values, speaker)


def head_pieces(value):
    over_y = send(value, ACROSS_Y)
    both = send(jnp.concatenate([value, over_y], axis=0), ACROSS_CORE)
    rows = value.shape[0]
    return [value, both[:rows], over_y, both[rows:]]


def plane_shards(video_rows, w_query, w_output, audio_tokens, w_key, w_value, row_lists, row_counts):
    rows, width = video_rows.shape
    block = w_query.shape[0]
    columns = w_query.shape[1]
    audio_width = audio_tokens.shape[2]
    ctx = lax.axis_index("ctx").astype(jnp.int32)
    h = lax.axis_index("head").astype(jnp.int32)
    z, x = ctx // 2, ctx % 2
    is_mid = (z == 1) | (z == 2)
    z_mid = jnp.where(is_mid, z, z ^ 1)

    query_weights = []
    first = 0
    for heads in QUERY_CHUNKS:
        size = heads * HD
        query_weights.append(
            jnp.concatenate(
                [
                    lax.dynamic_slice(w_query, (0, x * block + first), (block, size)),
                    lax.dynamic_slice(w_query, (0, (1 - x) * block + first), (block, size)),
                ],
                axis=1,
            )
        )
        first += size
    k_sizes = tuple(heads * HD for heads in QUERY_CHUNKS)

    def video_block(at):
        return lax.dynamic_slice(video_rows, (0, at * block), (rows, block))

    quarter_own = video_block(2 * (z_mid ^ h) + x)
    quarter_near = send(video_block(2 * (z_mid ^ h) + 1 - x), ACROSS_X)

    position = jnp.arange(rows, dtype=jnp.int32)
    named = (row_lists[:, :, None] == position[None, None, :]) & (
        position[None, :, None] < row_counts[:, :, None]
    )
    speaker_of = jnp.sum(
        jnp.any(named, axis=1) * jnp.array([[1], [2]], jnp.int32), axis=0
    ).astype(jnp.bfloat16)
    tokens = audio_tokens.shape[1]
    gathered = lax.all_gather(
        jnp.concatenate([audio_tokens.reshape(-1), speaker_of]), "ctx", axis=0
    )
    whole_audio = (
        gathered[:, : SPK * tokens * audio_width]
        .reshape(-1, SPK, tokens, audio_width)
        .transpose(1, 0, 2, 3)
        .reshape(-1, audio_width)
    )
    audio_length = whole_audio.shape[0] // SPK
    speakers = gathered[:, SPK * tokens * audio_width :].astype(jnp.int32)
    speaker_own = jnp.concatenate([speakers[ctx], speakers[ctx ^ 1]])[:, None]
    speaker_guest = jnp.concatenate([speakers[ctx ^ 2], speakers[ctx ^ 3]])[:, None]
    key_rows = add_rows(
        whole_audio, lax.dynamic_slice(w_key, (0, x * block), (audio_width, block))
    ).astype(jnp.bfloat16)
    value_rows = add_rows(
        whole_audio, lax.dynamic_slice(w_value, (0, x * block), (audio_width, block))
    ).astype(jnp.bfloat16)

    stacks = []
    for piece in query_weights:
        from_end = send(piece, END_TO_MID)
        from_mid = send(piece, MID_TO_MID)
        from_far = send(from_end, MID_TO_MID)
        stacks.append(jnp.stack([piece, from_end, from_far, from_mid]))

    guest = send(jnp.concatenate([quarter_own, quarter_near], axis=0), END_TO_MID)
    near_pieces = head_pieces(quarter_near)
    guest_pieces = head_pieces(guest)
    order = jnp.arange(4, dtype=jnp.int32) ^ h
    place = jnp.concatenate([order, 2 * (z_mid ^ order) + x])

    attended = []
    first = 0
    for stack, size in zip(stacks, k_sizes):
        at = slice(first, first + size)
        guest_kept, guest_sent = query_product(place, guest_pieces, stack, 2 * rows, False)
        guest_received = send(guest_sent, ACROSS_X)
        own_kept, own_sent = query_product(place, [video_rows] * 4, stack, rows, True)
        near_kept, near_sent = query_product(place, near_pieces, stack, rows, False)
        plane_received = send(jnp.concatenate([own_sent, near_sent], axis=0), ACROSS_X)
        guest_attended = attend(
            guest_kept, guest_received, key_rows[:, at], value_rows[:, at], speaker_guest, audio_length, True
        )
        from_mid = send(guest_attended, MID_TO_END)
        plane_attended = attend(
            jnp.concatenate([own_kept, near_kept], axis=0),
            plane_received,
            key_rows[:, at],
            value_rows[:, at],
            speaker_own,
            audio_length,
            True,
        )
        attended.append(head_pieces(jnp.where(is_mid, plane_attended, from_mid)))
        first += size

    out_place = order ^ z
    results = []
    first = 0
    for chunk in OUT_CHUNKS:
        size = chunk * HD
        piece = lax.slice_in_dim(w_output, first, first + size, axis=1)
        near = send(piece, SWAP_END)
        from_mid = send(piece, MID_TO_MID)
        from_far = send(near, MID_TO_MID)
        end_mid = send(from_mid, MID_TO_END)
        end_far = send(from_far, MID_TO_END)
        stack = jnp.stack(
            [
                piece,
                near,
                jnp.where(is_mid, from_far, end_mid),
                jnp.where(is_mid, from_mid, end_far),
            ]
        )
        lefts = [part for pieces in attended for part in pieces]
        total = out_product(out_place, lefts, stack, k_sizes)
        received = send(total[rows:], ACROSS_X)
        results.append((total[:rows] + received).astype(jnp.bfloat16))
        first += size
    return jnp.concatenate(results, axis=1)


def solution(mesh):
    in_specs = (
        P("ctx", None),
        P("ctx", "head"),
        P("ctx", "head"),
        P(None, "ctx", None),
        P(None, "head"),
        P(None, "head"),
        P(None, "ctx"),
        P(None, "ctx"),
    )
    out_specs = P("ctx", "head")
    planes = mesh.shape["ctx"] == 8 and mesh.shape["head"] == 4
    shards = plane_shards if planes else plain_shards
    return jax.shard_map(shards, mesh=mesh, in_specs=in_specs, out_specs=out_specs, check_vma=False)
```

```python
import functools

import jax
import jax.numpy as jnp
from jax import lax
from jax.experimental import pallas as pl
from jax.experimental.pallas import tpu as pltpu
from jax.sharding import PartitionSpec as P

HD = 128
SPK = 2
AXES = ("ctx", "head")
QUERY_CHUNKS = (3, 2)
OUT_CHUNKS = (6, 4)


def add_rows(left_rows, shard_piece):
    return jnp.dot(left_rows, shard_piece, preferred_element_type=jnp.float32)


def plain_shards(video_rows, w_query, w_output, audio_tokens, w_key, w_value, row_lists, row_counts):
    rows_dev = video_rows.shape[0]
    columns = w_query.shape[1]
    heads_dev = columns // HD
    queries = add_rows(video_rows, lax.all_gather(w_query, "ctx", axis=0, tiled=True)).astype(
        jnp.bfloat16
    )
    whole_audio = lax.all_gather(audio_tokens, "ctx", axis=1, tiled=True)
    key_rows = jnp.einsum(
        "sta,ad->std", whole_audio, w_key, preferred_element_type=jnp.float32
    ).astype(jnp.bfloat16)
    value_rows = jnp.einsum(
        "sta,ad->std", whole_audio, w_value, preferred_element_type=jnp.float32
    ).astype(jnp.bfloat16)
    audio_length = key_rows.shape[1]
    position = jnp.arange(rows_dev, dtype=jnp.int32)
    score_scale = 1.0 / HD**0.5
    summed = jnp.zeros((rows_dev, columns), jnp.float32)
    for speaker in range(SPK):
        target = row_lists[speaker]
        row_live = position < row_counts[speaker, 0]
        picked = queries[target].reshape(rows_dev, heads_dev, HD)
        key_block = key_rows[speaker].reshape(audio_length, heads_dev, HD)
        value_block = value_rows[speaker].reshape(audio_length, heads_dev, HD)
        scores = (
            jnp.einsum("rhd,khd->hrk", picked, key_block, preferred_element_type=jnp.float32)
            * score_scale
        )
        scores = scores - jnp.max(scores, axis=-1, keepdims=True)
        weights = jnp.exp(scores)
        weights = (weights / jnp.sum(weights, axis=-1, keepdims=True)).astype(jnp.bfloat16)
        blended = jnp.einsum(
            "hrk,khd->rhd", weights, value_block, preferred_element_type=jnp.float32
        ).astype(jnp.bfloat16)
        blended = blended.reshape(rows_dev, columns).astype(jnp.float32)
        blended = jnp.where(row_live[:, None], blended, jnp.zeros_like(blended))
        summed = summed.at[target].add(blended)
    attended = summed.astype(jnp.bfloat16)
    all_heads = lax.all_gather(attended, "head", axis=1, tiled=True)
    result = add_rows(all_heads, lax.all_gather(w_output, "ctx", axis=0, tiled=True))
    return result.astype(jnp.bfloat16)


def pairs(planes, move):
    found = []
    for z in range(planes):
        for x in range(2):
            for h in range(4):
                to = move(z, x, h)
                found.append(((2 * z + x) * 4 + h, (2 * to[0] + to[1]) * 4 + to[2]))
    return found


ACROSS_X = pairs(4, lambda z, x, h: (z, 1 - x, h))
ACROSS_Y = pairs(4, lambda z, x, h: (z, x, h ^ 2))
ACROSS_CORE = pairs(4, lambda z, x, h: (z, x, h ^ 1))
ONE_ALONG = pairs(4, lambda z, x, h: (z ^ 1, x, h))
TWO_ALONG = pairs(4, lambda z, x, h: (z ^ 2, x, h))
SAME_X = [[0, 2, 4, 6], [1, 3, 5, 7]]


def send(value, move):
    return lax.ppermute(value, AXES, move)


def along_z(value):
    return lax.all_gather(value, "ctx", axis=0, axis_index_groups=SAME_X)


def product(place, lefts, weights, k_sizes):
    total = None
    for j in range(4):
        first = 0
        for i, size in enumerate(k_sizes):
            right = weights[place[j], first : first + size, :]
            term = jnp.dot(lefts[i * 4 + j][...], right, preferred_element_type=jnp.float32)
            total = term if total is None else total + term
            first += size
    return total


def query_body(place, *refs):
    own, near = refs[:4], refs[4:8]
    weights, kept, sent = refs[8:]
    half = kept.shape[1]

    def write(lefts):
        total = product(place, lefts, weights, (weights.shape[1],))
        kept[...] = total[:, :half]
        sent[...] = total[:, half:]

    first_group = pl.program_id(0) < pl.num_programs(0) // 2
    pl.when(first_group)(lambda: write(own))
    pl.when(jnp.logical_not(first_group))(lambda: write(near))


def query_product(place, video_rows, near, weights):
    rows = video_rows.shape[0]
    depth, columns = weights.shape[1:]
    step = rows // 2
    own_specs = [
        pl.BlockSpec(
            (step, depth),
            functools.partial(lambda j, i, place: (jnp.minimum(i, 1), place[4 + j]), j),
        )
        for j in range(4)
    ]
    near_specs = [
        pl.BlockSpec((step, depth), lambda i, place: (jnp.maximum(i - 2, 0), 0)) for _ in range(4)
    ]
    half = columns // 2
    part = jax.ShapeDtypeStruct((2 * rows, half), jnp.float32)
    return pl.pallas_call(
        query_body,
        grid_spec=pltpu.PrefetchScalarGridSpec(
            num_scalar_prefetch=1,
            grid=(4,),
            in_specs=own_specs
            + near_specs
            + [pl.BlockSpec(weights.shape, lambda i, place: (0, 0, 0))],
            out_specs=[pl.BlockSpec((step, half), lambda i, place: (i, 0))] * 2,
        ),
        out_shape=[part, part],
        cost_estimate=pl.CostEstimate(
            flops=16 * rows * depth * columns,
            transcendentals=0,
            bytes_accessed=8 * (2 * rows + columns) * depth + 8 * rows * columns,
        ),
        name="query_product",
    )(place, *([video_rows] * 4), *near, weights)


def out_body(place, *refs, k_sizes):
    *lefts, weights, kept, sent = refs
    total = product(place, lefts, weights, k_sizes)
    pl.when(pl.program_id(0) < 2)(lambda: kept.__setitem__(..., total))
    pl.when(pl.program_id(0) >= 2)(lambda: sent.__setitem__(..., total))


def out_product(place, lefts, weights, k_sizes):
    rows = lefts[0].shape[0]
    columns = weights.shape[2]
    step = rows // 4
    left_specs = [
        pl.BlockSpec((step, size), lambda i, place: (i, 0)) for size in k_sizes for _ in range(4)
    ]
    part = jax.ShapeDtypeStruct((rows // 2, columns), jnp.float32)
    return pl.pallas_call(
        functools.partial(out_body, k_sizes=k_sizes),
        grid_spec=pltpu.PrefetchScalarGridSpec(
            num_scalar_prefetch=1,
            grid=(4,),
            in_specs=left_specs + [pl.BlockSpec(weights.shape, lambda i, place: (0, 0, 0))],
            out_specs=[
                pl.BlockSpec((step, columns), lambda i, place: (jnp.minimum(i, 1), 0)),
                pl.BlockSpec((step, columns), lambda i, place: (jnp.maximum(i - 2, 0), 0)),
            ],
        ),
        out_shape=[part, part],
        cost_estimate=pl.CostEstimate(
            flops=8 * rows * sum(k_sizes) * columns,
            transcendentals=0,
            bytes_accessed=8 * (rows + columns) * sum(k_sizes) + 4 * rows * columns,
        ),
        name="out_product",
    )(place, *lefts, weights)


def attend_body(kept, received, keys, values, speaker, attended, *, audio_length, heads):
    scale = 1.0 / HD**0.5
    of_row = speaker[...]
    lane = lax.broadcasted_iota(jnp.int32, (kept.shape[0], SPK * audio_length), 1)
    of_key = jnp.where(lane < audio_length, 1, 2)
    own_key = of_key == of_row
    live = of_row > 0
    for head in range(heads):
        at = slice(head * HD, (head + 1) * HD)
        query = (kept[:, at] + received[:, at]).astype(jnp.bfloat16)
        scores = (
            lax.dot_general(
                query, keys[:, at], (((1,), (1,)), ((), ())), preferred_element_type=jnp.float32
            )
            * scale
        )
        scores = jnp.where(own_key, scores, -1e30)
        scores = scores - jnp.max(scores, axis=-1, keepdims=True)
        weights = jnp.exp(scores)
        weights = (weights / jnp.sum(weights, axis=-1, keepdims=True)).astype(jnp.bfloat16)
        blended = jnp.dot(weights, values[:, at], preferred_element_type=jnp.float32)
        attended[:, at] = jnp.where(live, blended, 0.0).astype(jnp.bfloat16)


def attend(kept, received, keys, values, speaker, audio_length):
    rows, columns = kept.shape
    step = rows // 4
    at = lambda i: (i, 0)
    whole = pl.BlockSpec(keys.shape, lambda i: (0, 0))
    return pl.pallas_call(
        functools.partial(attend_body, audio_length=audio_length, heads=columns // HD),
        grid=(4,),
        in_specs=[
            pl.BlockSpec((step, columns), at),
            pl.BlockSpec((step, columns), lambda i: ((i + 2) % 4, 0)),
            whole,
            whole,
            pl.BlockSpec((step, 1), at),
        ],
        out_specs=pl.BlockSpec((step, columns), at),
        out_shape=jax.ShapeDtypeStruct((rows, columns), jnp.bfloat16),
        cost_estimate=pl.CostEstimate(
            flops=4 * rows * columns * SPK * audio_length,
            transcendentals=rows * SPK * audio_length * columns // HD,
            bytes_accessed=10 * rows * columns,
        ),
        name="attend",
    )(kept, received, keys, values, speaker)


def head_pieces(value):
    over_y = send(value, ACROSS_Y)
    return [value, send(value, ACROSS_CORE), over_y, send(over_y, ACROSS_CORE)]


def plane_shards(video_rows, w_query, w_output, audio_tokens, w_key, w_value, row_lists, row_counts):
    rows = video_rows.shape[0]
    block = w_query.shape[0]
    audio_width = audio_tokens.shape[2]
    ctx = lax.axis_index("ctx").astype(jnp.int32)
    h = lax.axis_index("head").astype(jnp.int32)
    x = ctx % 2
    k_sizes = tuple(heads * HD for heads in QUERY_CHUNKS)

    query_weights = []
    first = 0
    for size in k_sizes:
        query_weights.append(
            along_z(
                jnp.concatenate(
                    [
                        lax.dynamic_slice(w_query, (0, x * block + first), (block, size)),
                        lax.dynamic_slice(w_query, (0, (1 - x) * block + first), (block, size)),
                    ],
                    axis=1,
                )
            )
        )
        first += size

    near = head_pieces(
        send(
            lax.dynamic_slice(video_rows, (0, (2 * h + 1 - x) * block), (rows, block)), ACROSS_X
        )
    )
    order = jnp.arange(4, dtype=jnp.int32) ^ h
    place = jnp.concatenate([order, 2 * order + x])

    position = jnp.arange(rows, dtype=jnp.int32)
    named = (row_lists[:, :, None] == position[None, None, :]) & (
        position[None, :, None] < row_counts[:, :, None]
    )
    speaker_of = jnp.sum(
        jnp.any(named, axis=1) * jnp.array([[1], [2]], jnp.int32), axis=0
    ).astype(jnp.bfloat16)
    tokens = audio_tokens.shape[1]
    gathered = jnp.concatenate([audio_tokens.reshape(-1), speaker_of])[None]
    for move in (ACROSS_X, ONE_ALONG, TWO_ALONG):
        gathered = jnp.concatenate([gathered, send(gathered, move)], axis=0)
    whole_audio = (
        gathered[:, : SPK * tokens * audio_width]
        .reshape(-1, SPK, tokens, audio_width)
        .transpose(1, 0, 2, 3)
        .reshape(-1, audio_width)
    )
    audio_length = whole_audio.shape[0] // SPK
    speaker = gathered[:2, SPK * tokens * audio_width :].astype(jnp.int32).reshape(-1, 1)
    key_rows = add_rows(
        whole_audio, lax.dynamic_slice(w_key, (0, x * block), (audio_width, block))
    ).astype(jnp.bfloat16)
    value_rows = add_rows(
        whole_audio, lax.dynamic_slice(w_value, (0, x * block), (audio_width, block))
    ).astype(jnp.bfloat16)

    attended = []
    first = 0
    for weights, size in zip(query_weights, k_sizes):
        at = slice(first, first + size)
        kept, sent = query_product(place, video_rows, near, weights)
        received = send(sent, ACROSS_X)
        attended += head_pieces(
            attend(kept, received, key_rows[:, at], value_rows[:, at], speaker, audio_length)
        )
        first += size

    results = []
    first = 0
    for heads in OUT_CHUNKS:
        size = heads * HD
        weights = along_z(lax.slice_in_dim(w_output, first, first + size, axis=1))
        kept, sent = out_product(place, attended, weights, k_sizes)
        results.append((kept + send(sent, ACROSS_X)).astype(jnp.bfloat16))
        first += size
    return jnp.concatenate(results, axis=1)


def solution(mesh):
    in_specs = (
        P("ctx", None),
        P("ctx", "head"),
        P("ctx", "head"),
        P(None, "ctx", None),
        P(None, "head"),
        P(None, "head"),
        P(None, "ctx"),
        P(None, "ctx"),
    )
    out_specs = P("ctx", "head")
    planes = mesh.shape["ctx"] == 8 and mesh.shape["head"] == 4
    shards = plane_shards if planes else plain_shards
    return jax.shard_map(shards, mesh=mesh, in_specs=in_specs, out_specs=out_specs, check_vma=False)
```

```python
import functools

import jax
import jax.numpy as jnp
from jax import lax
from jax.experimental import pallas as pl
from jax.experimental.pallas import tpu as pltpu
from jax.sharding import PartitionSpec as P

HD = 128
SPK = 2
AXES = ("ctx", "head")
OUT_CHUNKS = (7, 3)


def add_rows(left_rows, shard_piece):
    return jnp.dot(left_rows, shard_piece, preferred_element_type=jnp.float32)


def plain_shards(video_rows, w_query, w_output, audio_tokens, w_key, w_value, row_lists, row_counts):
    rows_dev = video_rows.shape[0]
    columns = w_query.shape[1]
    heads_dev = columns // HD
    queries = add_rows(video_rows, lax.all_gather(w_query, "ctx", axis=0, tiled=True)).astype(
        jnp.bfloat16
    )
    whole_audio = lax.all_gather(audio_tokens, "ctx", axis=1, tiled=True)
    key_rows = jnp.einsum(
        "sta,ad->std", whole_audio, w_key, preferred_element_type=jnp.float32
    ).astype(jnp.bfloat16)
    value_rows = jnp.einsum(
        "sta,ad->std", whole_audio, w_value, preferred_element_type=jnp.float32
    ).astype(jnp.bfloat16)
    audio_length = key_rows.shape[1]
    position = jnp.arange(rows_dev, dtype=jnp.int32)
    score_scale = 1.0 / HD**0.5
    summed = jnp.zeros((rows_dev, columns), jnp.float32)
    for speaker in range(SPK):
        target = row_lists[speaker]
        row_live = position < row_counts[speaker, 0]
        picked = queries[target].reshape(rows_dev, heads_dev, HD)
        key_block = key_rows[speaker].reshape(audio_length, heads_dev, HD)
        value_block = value_rows[speaker].reshape(audio_length, heads_dev, HD)
        scores = (
            jnp.einsum("rhd,khd->hrk", picked, key_block, preferred_element_type=jnp.float32)
            * score_scale
        )
        scores = scores - jnp.max(scores, axis=-1, keepdims=True)
        weights = jnp.exp(scores)
        weights = (weights / jnp.sum(weights, axis=-1, keepdims=True)).astype(jnp.bfloat16)
        blended = jnp.einsum(
            "hrk,khd->rhd", weights, value_block, preferred_element_type=jnp.float32
        ).astype(jnp.bfloat16)
        blended = blended.reshape(rows_dev, columns).astype(jnp.float32)
        blended = jnp.where(row_live[:, None], blended, jnp.zeros_like(blended))
        summed = summed.at[target].add(blended)
    attended = summed.astype(jnp.bfloat16)
    all_heads = lax.all_gather(attended, "head", axis=1, tiled=True)
    result = add_rows(all_heads, lax.all_gather(w_output, "ctx", axis=0, tiled=True))
    return result.astype(jnp.bfloat16)


def pairs(planes, move):
    found = []
    for z in range(planes):
        for x in range(2):
            for h in range(4):
                to = move(z, x, h)
                found.append(((2 * z + x) * 4 + h, (2 * to[0] + to[1]) * 4 + to[2]))
    return found


ACROSS_X = pairs(4, lambda z, x, h: (z, 1 - x, h))
ACROSS_Y = pairs(4, lambda z, x, h: (z, x, h ^ 2))
ACROSS_CORE = pairs(4, lambda z, x, h: (z, x, h ^ 1))
ONE_ALONG = pairs(4, lambda z, x, h: (z ^ 1, x, h))
TWO_ALONG = pairs(4, lambda z, x, h: (z ^ 2, x, h))
SAME_X = [[0, 2, 4, 6], [1, 3, 5, 7]]


def send(value, move):
    return lax.ppermute(value, AXES, move)


def along_z(value):
    return lax.all_gather(value, "ctx", axis=0, axis_index_groups=SAME_X)


def query_body(place, *refs):
    *lefts, keep_weights, send_weights, kept, sent = refs
    if len(lefts) == 4:
        values = [left[...] for left in lefts]
        lefts = [jnp.concatenate(values[:2], axis=1), jnp.concatenate(values[2:], axis=1)]
    else:
        lefts = [left[...] for left in lefts]

    def total(weights):
        first = jnp.dot(lefts[0], weights[place[0]], preferred_element_type=jnp.float32)
        second = jnp.dot(lefts[1], weights[place[1]], preferred_element_type=jnp.float32)
        return first + second

    kept[...] = total(keep_weights)
    sent[...] = total(send_weights)


def query_product(place, lefts, weights):
    rows = lefts[0].shape[0]
    depth, columns = weights.shape[1:]
    step = rows // 2
    half = columns // 2
    if len(lefts) == 1:
        left_specs = [
            pl.BlockSpec((step, depth // 2), functools.partial(lambda j, i, place: (i, place[4 + j]), j))
            for j in range(4)
        ]
        lefts = lefts * 4
    else:
        left_specs = [pl.BlockSpec((step, depth), lambda i, place: (i, 0))] * 2
    part = jax.ShapeDtypeStruct((rows, half), jnp.float32)
    return pl.pallas_call(
        query_body,
        grid_spec=pltpu.PrefetchScalarGridSpec(
            num_scalar_prefetch=1,
            grid=(2,),
            in_specs=left_specs
            + [
                pl.BlockSpec((2, depth, half), lambda i, place: (0, 0, place[2])),
                pl.BlockSpec((2, depth, half), lambda i, place: (0, 0, place[3])),
            ],
            out_specs=[pl.BlockSpec((step, half), lambda i, place: (i, 0))] * 2,
        ),
        out_shape=[part, part],
        cost_estimate=pl.CostEstimate(
            flops=4 * rows * depth * columns,
            transcendentals=0,
            bytes_accessed=4 * (rows + columns) * depth + 4 * rows * columns,
        ),
        name="query_product",
    )(place, *lefts, weights, weights)


def out_product(place, groups, weights):
    rows, depth = groups[0][0].shape
    columns = weights.shape[2]
    step = rows // 2

    def body(place, *refs):
        own, near, rest = refs[:4], refs[4:8], refs[8:]
        weights, kept, sent = rest

        def total(lefts):
            found = None
            for j in range(4):
                term = jnp.dot(lefts[j][...], weights[place[j]], preferred_element_type=jnp.float32)
                found = term if found is None else found + term
            return found

        pl.when(pl.program_id(0) < 2)(lambda: sent.__setitem__(..., total(near)))
        pl.when(pl.program_id(0) >= 2)(lambda: kept.__setitem__(..., total(own)))

    early = lambda i: jnp.minimum(i, 1)
    late = lambda i: jnp.maximum(i - 2, 0)
    specs = lambda at: [
        pl.BlockSpec(
            (step, depth), functools.partial(lambda skip, i, place: (at(i) + skip, 0), skip)
        )
        for skip in (0, 0, 0, 2)
    ]
    pieces = [piece for own, core, over_y in groups for piece in (own, core, over_y, core)]
    part = jax.ShapeDtypeStruct((rows, columns), jnp.float32)
    return pl.pallas_call(
        body,
        grid_spec=pltpu.PrefetchScalarGridSpec(
            num_scalar_prefetch=1,
            grid=(4,),
            in_specs=specs(late)
            + specs(early)
            + [pl.BlockSpec(weights.shape, lambda i, place: (0, 0, 0))],
            out_specs=[
                pl.BlockSpec((step, columns), lambda i, place: (late(i), 0)),
                pl.BlockSpec((step, columns), lambda i, place: (early(i), 0)),
            ],
        ),
        out_shape=[part, part],
        cost_estimate=pl.CostEstimate(
            flops=16 * rows * depth * columns,
            transcendentals=0,
            bytes_accessed=8 * (2 * rows + columns) * depth + 8 * rows * columns,
        ),
        name="out_product",
    )(place, *pieces, weights)


def attend_body(kept, received, keys, values, speaker, attended, *, audio_length, heads):
    scale = 1.0 / HD**0.5
    of_row = speaker[...]
    lane = lax.broadcasted_iota(jnp.int32, (kept.shape[0], SPK * audio_length), 1)
    of_key = jnp.where(lane < audio_length, 1, 2)
    own_key = of_key == of_row
    live = of_row > 0
    for head in range(heads):
        at = slice(head * HD, (head + 1) * HD)
        query = (kept[:, at] + received[:, at]).astype(jnp.bfloat16)
        scores = (
            lax.dot_general(
                query, keys[:, at], (((1,), (1,)), ((), ())), preferred_element_type=jnp.float32
            )
            * scale
        )
        scores = jnp.where(own_key, scores, -1e30)
        scores = scores - jnp.max(scores, axis=-1, keepdims=True)
        weights = jnp.exp(scores)
        weights = (weights / jnp.sum(weights, axis=-1, keepdims=True)).astype(jnp.bfloat16)
        blended = jnp.dot(weights, values[:, at], preferred_element_type=jnp.float32)
        attended[:, at] = jnp.where(live, blended, 0.0).astype(jnp.bfloat16)


def attend(kept, received, keys, values, speaker, audio_length):
    rows, columns = kept.shape
    step = rows // 2
    at = lambda i: (i, 0)
    whole = pl.BlockSpec(keys.shape, lambda i: (0, 0))
    return pl.pallas_call(
        functools.partial(attend_body, audio_length=audio_length, heads=columns // HD),
        grid=(2,),
        in_specs=[
            pl.BlockSpec((step, columns), at),
            pl.BlockSpec((step, columns), at),
            whole,
            whole,
            pl.BlockSpec((step, 1), at),
        ],
        out_specs=pl.BlockSpec((step, columns), at),
        out_shape=jax.ShapeDtypeStruct((rows, columns), jnp.bfloat16),
        cost_estimate=pl.CostEstimate(
            flops=4 * rows * columns * SPK * audio_length,
            transcendentals=rows * SPK * audio_length * columns // HD,
            bytes_accessed=10 * rows * columns,
        ),
        name="attend",
    )(kept, received, keys, values, speaker)


def head_pieces(value):
    over_y = send(value, ACROSS_Y)
    return value, send(jnp.concatenate([value, over_y], axis=0), ACROSS_CORE), over_y


def plane_shards(video_rows, w_query, w_output, audio_tokens, w_key, w_value, row_lists, row_counts):
    rows = video_rows.shape[0]
    block = w_query.shape[0]
    audio_width = audio_tokens.shape[2]
    ctx = lax.axis_index("ctx").astype(jnp.int32)
    h = lax.axis_index("head").astype(jnp.int32)
    x = ctx % 2
    core = h % 2

    query_weights = along_z(w_query).reshape(2, 2 * block, -1)

    near_block = lambda plane: lax.dynamic_slice(
        video_rows, (0, (2 * plane + 1 - x) * block), (rows, block)
    )
    near_half = send(
        jnp.concatenate([near_block(2 * core), near_block(2 * core + 1)], axis=1), ACROSS_X
    )
    near = [near_half, send(near_half, ACROSS_CORE)]
    planes = jnp.arange(4, dtype=jnp.int32)
    sides = jnp.stack([x, 1 - x])
    near_place = jnp.concatenate([jnp.stack([core, 1 - core]), sides])
    own_place = jnp.concatenate([planes[:2], sides, 2 * planes + x])

    position = jnp.arange(rows, dtype=jnp.int32)
    named = (row_lists[:, :, None] == position[None, None, :]) & (
        position[None, :, None] < row_counts[:, :, None]
    )
    speaker_of = jnp.sum(
        jnp.any(named, axis=1) * jnp.array([[1], [2]], jnp.int32), axis=0
    ).astype(jnp.bfloat16)
    tokens = audio_tokens.shape[1]
    gathered = jnp.concatenate([audio_tokens.reshape(-1), speaker_of])[None]
    for move in (ACROSS_X, ONE_ALONG, TWO_ALONG):
        gathered = jnp.concatenate([gathered, send(gathered, move)], axis=0)
    whole_audio = (
        gathered[:, : SPK * tokens * audio_width]
        .reshape(-1, SPK, tokens, audio_width)
        .transpose(1, 0, 2, 3)
        .reshape(-1, audio_width)
    )
    audio_length = whole_audio.shape[0] // SPK
    speakers = gathered[:2, SPK * tokens * audio_width :].astype(jnp.int32)
    own_block = lambda weights: lax.dynamic_slice(weights, (0, x * block), (audio_width, block))
    key_rows = add_rows(whole_audio, own_block(w_key)).astype(jnp.bfloat16)
    value_rows = add_rows(whole_audio, own_block(w_value)).astype(jnp.bfloat16)

    near_kept, near_sent = query_product(near_place, near, query_weights)
    own_received = send(near_sent, ACROSS_X)
    own_kept, own_sent = query_product(own_place, [video_rows], query_weights)
    near_received = send(own_sent, ACROSS_X)
    attended = [
        head_pieces(
            attend(kept, received, key_rows, value_rows, speakers[side][:, None], audio_length)
        )
        for side, kept, received in ((0, own_kept, own_received), (1, near_kept, near_received))
    ]

    results = []
    first = 0
    for heads in OUT_CHUNKS:
        size = heads * HD
        weights = along_z(lax.slice_in_dim(w_output, first, first + size, axis=1))
        kept, sent = out_product(planes ^ h, attended, weights)
        results.append((kept + send(sent, ACROSS_X)).astype(jnp.bfloat16))
        first += size
    return jnp.concatenate(results, axis=1)


def solution(mesh):
    in_specs = (
        P("ctx", None),
        P("ctx", "head"),
        P("ctx", "head"),
        P(None, "ctx", None),
        P(None, "head"),
        P(None, "head"),
        P(None, "ctx"),
        P(None, "ctx"),
    )
    out_specs = P("ctx", "head")
    planes = mesh.shape["ctx"] == 8 and mesh.shape["head"] == 4
    shards = plane_shards if planes else plain_shards
    return jax.shard_map(shards, mesh=mesh, in_specs=in_specs, out_specs=out_specs, check_vma=False)
```

```python
import functools

import jax
import jax.numpy as jnp
from jax import lax
from jax.experimental import pallas as pl
from jax.experimental.pallas import tpu as pltpu
from jax.sharding import PartitionSpec as P

HD = 128
SPK = 2
AXES = ("ctx", "head")
HOPPED = 2
GATHERED = (6, 2)


def add_rows(left_rows, shard_piece):
    return jnp.dot(left_rows, shard_piece, preferred_element_type=jnp.float32)


def plain_shards(video_rows, w_query, w_output, audio_tokens, w_key, w_value, row_lists, row_counts):
    rows_dev = video_rows.shape[0]
    columns = w_query.shape[1]
    heads_dev = columns // HD
    queries = add_rows(video_rows, lax.all_gather(w_query, "ctx", axis=0, tiled=True)).astype(
        jnp.bfloat16
    )
    whole_audio = lax.all_gather(audio_tokens, "ctx", axis=1, tiled=True)
    key_rows = jnp.einsum(
        "sta,ad->std", whole_audio, w_key, preferred_element_type=jnp.float32
    ).astype(jnp.bfloat16)
    value_rows = jnp.einsum(
        "sta,ad->std", whole_audio, w_value, preferred_element_type=jnp.float32
    ).astype(jnp.bfloat16)
    audio_length = key_rows.shape[1]
    position = jnp.arange(rows_dev, dtype=jnp.int32)
    score_scale = 1.0 / HD**0.5
    summed = jnp.zeros((rows_dev, columns), jnp.float32)
    for speaker in range(SPK):
        target = row_lists[speaker]
        row_live = position < row_counts[speaker, 0]
        picked = queries[target].reshape(rows_dev, heads_dev, HD)
        key_block = key_rows[speaker].reshape(audio_length, heads_dev, HD)
        value_block = value_rows[speaker].reshape(audio_length, heads_dev, HD)
        scores = (
            jnp.einsum("rhd,khd->hrk", picked, key_block, preferred_element_type=jnp.float32)
            * score_scale
        )
        scores = scores - jnp.max(scores, axis=-1, keepdims=True)
        weights = jnp.exp(scores)
        weights = (weights / jnp.sum(weights, axis=-1, keepdims=True)).astype(jnp.bfloat16)
        blended = jnp.einsum(
            "hrk,khd->rhd", weights, value_block, preferred_element_type=jnp.float32
        ).astype(jnp.bfloat16)
        blended = blended.reshape(rows_dev, columns).astype(jnp.float32)
        blended = jnp.where(row_live[:, None], blended, jnp.zeros_like(blended))
        summed = summed.at[target].add(blended)
    attended = summed.astype(jnp.bfloat16)
    all_heads = lax.all_gather(attended, "head", axis=1, tiled=True)
    result = add_rows(all_heads, lax.all_gather(w_output, "ctx", axis=0, tiled=True))
    return result.astype(jnp.bfloat16)


def pairs(planes, move):
    found = []
    for z in range(planes):
        for x in range(2):
            for h in range(4):
                to = move(z, x, h)
                found.append(((2 * z + x) * 4 + h, (2 * to[0] + to[1]) * 4 + to[2]))
    return found


ACROSS_X = pairs(4, lambda z, x, h: (z, 1 - x, h))
ACROSS_Y = pairs(4, lambda z, x, h: (z, x, h ^ 2))
ACROSS_CORE = pairs(4, lambda z, x, h: (z, x, h ^ 1))
ONE_ALONG = pairs(4, lambda z, x, h: (z ^ 1, x, h))
TWO_ALONG = pairs(4, lambda z, x, h: (z ^ 2, x, h))
MID_TO_END = [pair for pair in ONE_ALONG if pair[0] // 8 in (1, 2)]
MID_TO_MID = pairs(4, lambda z, x, h: (3 - z if z in (1, 2) else z, x, h))
SAME_X = [[0, 2, 4, 6], [1, 3, 5, 7]]


def send(value, move):
    return lax.ppermute(value, AXES, move)


def along_z(value):
    return lax.all_gather(value, "ctx", axis=0, axis_index_groups=SAME_X)


def diagonal(groups):
    shape = (groups * 128, 128)
    row = lax.broadcasted_iota(jnp.int32, shape, 0) % 128
    return row == lax.broadcasted_iota(jnp.int32, shape, 1)


def pack(value, packed):
    rows, columns = value.shape
    groups = rows // 128
    peak = jnp.max(jnp.abs(value), axis=1, keepdims=True)
    power = jnp.clip(jnp.floor(jnp.log2(jnp.maximum(peak, 1e-30))) + 1.0, -90.0, 120.0)
    scaled = jnp.clip(jnp.round(value * jnp.exp2(15.0 - power)), -32767.0, 32767.0)
    packed[:rows, :] = scaled.astype(jnp.int32).astype(jnp.int16)
    spread = jnp.where(diagonal(groups), power, 0.0).reshape(groups, 128, 128).sum(axis=1)
    spread = jnp.concatenate([spread, jnp.zeros((16 - groups, 128), jnp.float32)], axis=0)
    packed[rows:, :128] = spread.astype(jnp.int32).astype(jnp.int16)
    packed[rows:, 128:] = jnp.zeros((16, columns - 128), jnp.int16)


def row_scale(packed):
    groups = (packed.shape[0] - 16) // 128
    spread = packed[groups * 128 :, :128].astype(jnp.int32).astype(jnp.float32)[:groups]
    spread = jnp.broadcast_to(spread[:, None, :], (groups, 128, 128)).reshape(groups * 128, 128)
    power = jnp.sum(jnp.where(diagonal(groups), spread, 0.0), axis=1, keepdims=True)
    return jnp.exp2(power - 15.0)


def unpack(packed, at, scale):
    return packed[: packed.shape[0] - 16, at].astype(jnp.int32).astype(jnp.float32) * scale


def query_body(place, *refs):
    *lefts, keep_weights, send_weights, kept, sent = refs
    if len(lefts) == 4:
        values = [left[...] for left in lefts]
        lefts = [jnp.concatenate(values[:2], axis=1), jnp.concatenate(values[2:], axis=1)]
    else:
        lefts = [left[...] for left in lefts]

    def total(weights):
        first = jnp.dot(lefts[0], weights[place[0]], preferred_element_type=jnp.float32)
        second = jnp.dot(lefts[1], weights[place[1]], preferred_element_type=jnp.float32)
        return first + second

    kept[...] = total(keep_weights)
    pack(total(send_weights), sent)


def query_product(place, lefts, weights):
    rows = lefts[0].shape[0]
    depth, columns = weights.shape[1:]
    step = rows // 2
    half = columns // 2
    if len(lefts) == 1:
        left_specs = [
            pl.BlockSpec((step, depth // 2), functools.partial(lambda j, i, place: (i, place[4 + j]), j))
            for j in range(4)
        ]
        lefts = lefts * 4
    else:
        left_specs = [pl.BlockSpec((step, depth), lambda i, place: (i, 0))] * 2
    out_shape = [
        jax.ShapeDtypeStruct((rows, half), jnp.float32),
        jax.ShapeDtypeStruct((2 * (step + 16), half), jnp.int16),
    ]
    return pl.pallas_call(
        query_body,
        grid_spec=pltpu.PrefetchScalarGridSpec(
            num_scalar_prefetch=1,
            grid=(2,),
            in_specs=left_specs
            + [
                pl.BlockSpec((2, depth, half), lambda i, place: (0, 0, place[2])),
                pl.BlockSpec((2, depth, half), lambda i, place: (0, 0, place[3])),
            ],
            out_specs=[
                pl.BlockSpec((step, half), lambda i, place: (i, 0)),
                pl.BlockSpec((step + 16, half), lambda i, place: (i, 0)),
            ],
        ),
        out_shape=out_shape,
        cost_estimate=pl.CostEstimate(
            flops=4 * rows * depth * columns,
            transcendentals=0,
            bytes_accessed=4 * (rows + columns) * depth + 4 * rows * columns,
        ),
        name="query_product",
    )(place, *lefts, weights, weights)


def out_product(place, groups, weights):
    rows, depth = groups[0][0].shape
    columns = weights.shape[2]
    step = rows // 2

    def body(place, *refs):
        own, near, rest = refs[:4], refs[4:8], refs[8:]
        weights, kept, sent = rest

        def total(lefts):
            found = None
            for j in range(4):
                term = jnp.dot(lefts[j][...], weights[place[j]], preferred_element_type=jnp.float32)
                found = term if found is None else found + term
            return found

        pl.when(pl.program_id(0) < 2)(lambda: pack(total(near), sent))
        pl.when(pl.program_id(0) >= 2)(lambda: kept.__setitem__(..., total(own)))

    early = lambda i: jnp.minimum(i, 1)
    late = lambda i: jnp.maximum(i - 2, 0)
    specs = lambda at: [
        pl.BlockSpec(
            (step, depth), functools.partial(lambda skip, i, place: (at(i) + skip, 0), skip)
        )
        for skip in (0, 0, 0, 2)
    ]
    pieces = [piece for own, core, over_y in groups for piece in (own, core, over_y, core)]
    out_shape = [
        jax.ShapeDtypeStruct((rows, columns), jnp.float32),
        jax.ShapeDtypeStruct((2 * (step + 16), columns), jnp.int16),
    ]
    return pl.pallas_call(
        body,
        grid_spec=pltpu.PrefetchScalarGridSpec(
            num_scalar_prefetch=1,
            grid=(4,),
            in_specs=specs(late)
            + specs(early)
            + [pl.BlockSpec(weights.shape, lambda i, place: (0, 0, 0))],
            out_specs=[
                pl.BlockSpec((step, columns), lambda i, place: (late(i), 0)),
                pl.BlockSpec((step + 16, columns), lambda i, place: (early(i), 0)),
            ],
        ),
        out_shape=out_shape,
        cost_estimate=pl.CostEstimate(
            flops=16 * rows * depth * columns,
            transcendentals=0,
            bytes_accessed=8 * (2 * rows + columns) * depth + 8 * rows * columns,
        ),
        name="out_product",
    )(place, *pieces, weights)


def attend_body(kept, received, keys, values, speaker, attended, *, audio_length, heads):
    scale = 1.0 / HD**0.5
    of_row = speaker[...]
    lane = lax.broadcasted_iota(jnp.int32, (kept.shape[0], SPK * audio_length), 1)
    of_key = jnp.where(lane < audio_length, 1, 2)
    own_key = of_key == of_row
    live = of_row > 0
    received_scale = row_scale(received)
    for head in range(heads):
        at = slice(head * HD, (head + 1) * HD)
        query = (kept[:, at] + unpack(received, at, received_scale)).astype(jnp.bfloat16)
        scores = (
            lax.dot_general(
                query, keys[:, at], (((1,), (1,)), ((), ())), preferred_element_type=jnp.float32
            )
            * scale
        )
        scores = jnp.where(own_key, scores, -1e30)
        scores = scores - jnp.max(scores, axis=-1, keepdims=True)
        weights = jnp.exp(scores)
        weights = (weights / jnp.sum(weights, axis=-1, keepdims=True)).astype(jnp.bfloat16)
        blended = jnp.dot(weights, values[:, at], preferred_element_type=jnp.float32)
        attended[:, at] = jnp.where(live, blended, 0.0).astype(jnp.bfloat16)


def attend(kept, received, keys, values, speaker, audio_length):
    rows, columns = kept.shape
    step = rows // 2
    at = lambda i: (i, 0)
    whole = pl.BlockSpec(keys.shape, lambda i: (0, 0))
    return pl.pallas_call(
        functools.partial(attend_body, audio_length=audio_length, heads=columns // HD),
        grid=(2,),
        in_specs=[
            pl.BlockSpec((step, columns), at),
            pl.BlockSpec((step + 16, columns), at),
            whole,
            whole,
            pl.BlockSpec((step, 1), at),
        ],
        out_specs=pl.BlockSpec((step, columns), at),
        out_shape=jax.ShapeDtypeStruct((rows, columns), jnp.bfloat16),
        cost_estimate=pl.CostEstimate(
            flops=4 * rows * columns * SPK * audio_length,
            transcendentals=rows * SPK * audio_length * columns // HD,
            bytes_accessed=10 * rows * columns,
        ),
        name="attend",
    )(kept, received, keys, values, speaker)


def finish_body(kept, received, scales, *refs):
    refs[-1][...] = (kept[...] + unpack(received, slice(None), row_scale(scales))).astype(
        jnp.bfloat16
    )


def finish(kept, received, first, whole, result):
    rows, columns = kept.shape
    step = rows // 2
    width = 2 * HD
    at = lambda i, j: (i, j)
    given = [] if result is None else [result]
    return pl.pallas_call(
        finish_body,
        grid=(2, columns // width),
        in_specs=[
            pl.BlockSpec((step, width), at),
            pl.BlockSpec((step + 16, width), at),
            pl.BlockSpec((step + 16, 128), lambda i, j: (i, 0)),
        ]
        + [pl.BlockSpec(memory_space=pl.ANY)] * len(given),
        out_specs=pl.BlockSpec((step, width), lambda i, j: (i, first // width + j)),
        out_shape=jax.ShapeDtypeStruct((rows, whole), jnp.bfloat16),
        input_output_aliases={3: 0} if given else {},
        cost_estimate=pl.CostEstimate(
            flops=2 * rows * columns, transcendentals=0, bytes_accessed=8 * rows * columns
        ),
        name="finish",
    )(kept, received, received, *given)


def head_pieces(value):
    over_y = send(value, ACROSS_Y)
    return value, send(jnp.concatenate([value, over_y], axis=0), ACROSS_CORE), over_y


def plane_shards(video_rows, w_query, w_output, audio_tokens, w_key, w_value, row_lists, row_counts):
    rows = video_rows.shape[0]
    block = w_query.shape[0]
    audio_width = audio_tokens.shape[2]
    ctx = lax.axis_index("ctx").astype(jnp.int32)
    h = lax.axis_index("head").astype(jnp.int32)
    x = ctx % 2
    core = h % 2

    query_weights = along_z(w_query).reshape(2, 2 * block, -1)

    z = ctx // 2
    is_mid = (z == 1) | (z == 2)
    hopped = HOPPED * HD
    if hopped:
        piece = w_output[:, :hopped]
        swapped = send(piece, ONE_ALONG)
        opposite = send(piece, MID_TO_MID)
        last = send(swapped, MID_TO_MID)
        to_end = send(opposite, MID_TO_END)
        last_to_end = send(last, MID_TO_END)
        third = jnp.where(is_mid, last, to_end)
        fourth = jnp.where(is_mid, opposite, last_to_end)
        hopped_weights = jnp.stack([piece, swapped, third, fourth])
        query_weights, hopped_weights = lax.optimization_barrier((query_weights, hopped_weights))

    near_block = lambda plane: lax.dynamic_slice(
        video_rows, (0, (2 * plane + 1 - x) * block), (rows, block)
    )
    near_half = send(
        jnp.concatenate([near_block(2 * core), near_block(2 * core + 1)], axis=1), ACROSS_X
    )
    near = [near_half, send(near_half, ACROSS_CORE)]
    planes = jnp.arange(4, dtype=jnp.int32)
    sides = jnp.stack([x, 1 - x])
    near_place = jnp.concatenate([jnp.stack([core, 1 - core]), sides])
    own_place = jnp.concatenate([planes[:2], sides, 2 * planes + x])

    position = jnp.arange(rows, dtype=jnp.int32)
    named = (row_lists[:, :, None] == position[None, None, :]) & (
        position[None, :, None] < row_counts[:, :, None]
    )
    speaker_of = jnp.sum(
        jnp.any(named, axis=1) * jnp.array([[1], [2]], jnp.int32), axis=0
    ).astype(jnp.bfloat16)
    tokens = audio_tokens.shape[1]
    gathered = jnp.concatenate([audio_tokens.reshape(-1), speaker_of])[None]
    for move in (ACROSS_X, ONE_ALONG, TWO_ALONG):
        gathered = jnp.concatenate([gathered, send(gathered, move)], axis=0)
    whole_audio = (
        gathered[:, : SPK * tokens * audio_width]
        .reshape(-1, SPK, tokens, audio_width)
        .transpose(1, 0, 2, 3)
        .reshape(-1, audio_width)
    )
    audio_length = whole_audio.shape[0] // SPK
    speakers = gathered[:2, SPK * tokens * audio_width :].astype(jnp.int32)
    own_block = lambda weights: lax.dynamic_slice(weights, (0, x * block), (audio_width, block))
    key_rows = add_rows(whole_audio, own_block(w_key)).astype(jnp.bfloat16)
    value_rows = add_rows(whole_audio, own_block(w_value)).astype(jnp.bfloat16)

    near_kept, near_sent = query_product(near_place, near, query_weights)
    own_received = send(near_sent, ACROSS_X)
    own_kept, own_sent = query_product(own_place, [video_rows], query_weights)
    near_received = send(own_sent, ACROSS_X)
    attended = [
        head_pieces(
            attend(kept, received, key_rows, value_rows, speakers[side][:, None], audio_length)
        )
        for side, kept, received in ((0, own_kept, own_received), (1, near_kept, near_received))
    ]

    chunks = [(hopped_weights, planes ^ h ^ z, 0)] if hopped else []
    first = hopped
    for heads in GATHERED:
        size = heads * HD
        chunks.append((along_z(w_output[:, first : first + size]), planes ^ h, first))
        first += size
    result = None
    for weights, out_place, first in chunks:
        kept, sent = out_product(out_place, attended, weights)
        result = finish(kept, send(sent, ACROSS_X), first, w_output.shape[1], result)
    return result


def solution(mesh):
    in_specs = (
        P("ctx", None),
        P("ctx", "head"),
        P("ctx", "head"),
        P(None, "ctx", None),
        P(None, "head"),
        P(None, "head"),
        P(None, "ctx"),
        P(None, "ctx"),
    )
    out_specs = P("ctx", "head")
    planes = mesh.shape["ctx"] == 8 and mesh.shape["head"] == 4
    shards = plane_shards if planes else plain_shards
    return jax.shard_map(shards, mesh=mesh, in_specs=in_specs, out_specs=out_specs, check_vma=False)
```

```python
import functools

import jax
import jax.numpy as jnp
from jax import lax
from jax.experimental import pallas as pl
from jax.experimental.pallas import tpu as pltpu
from jax.sharding import PartitionSpec as P

HD = 128
SPK = 2
AXES = ("ctx", "head")
GATHERED_HEADS = 3
OUT_CHUNKS = (8, 2)


def add_rows(left_rows, shard_piece):
    return jnp.dot(left_rows, shard_piece, preferred_element_type=jnp.float32)


def plain_shards(video_rows, w_query, w_output, audio_tokens, w_key, w_value, row_lists, row_counts):
    rows_dev = video_rows.shape[0]
    columns = w_query.shape[1]
    heads_dev = columns // HD
    queries = add_rows(video_rows, lax.all_gather(w_query, "ctx", axis=0, tiled=True)).astype(
        jnp.bfloat16
    )
    whole_audio = lax.all_gather(audio_tokens, "ctx", axis=1, tiled=True)
    key_rows = jnp.einsum(
        "sta,ad->std", whole_audio, w_key, preferred_element_type=jnp.float32
    ).astype(jnp.bfloat16)
    value_rows = jnp.einsum(
        "sta,ad->std", whole_audio, w_value, preferred_element_type=jnp.float32
    ).astype(jnp.bfloat16)
    audio_length = key_rows.shape[1]
    position = jnp.arange(rows_dev, dtype=jnp.int32)
    score_scale = 1.0 / HD**0.5
    summed = jnp.zeros((rows_dev, columns), jnp.float32)
    for speaker in range(SPK):
        target = row_lists[speaker]
        row_live = position < row_counts[speaker, 0]
        picked = queries[target].reshape(rows_dev, heads_dev, HD)
        key_block = key_rows[speaker].reshape(audio_length, heads_dev, HD)
        value_block = value_rows[speaker].reshape(audio_length, heads_dev, HD)
        scores = (
            jnp.einsum("rhd,khd->hrk", picked, key_block, preferred_element_type=jnp.float32)
            * score_scale
        )
        scores = scores - jnp.max(scores, axis=-1, keepdims=True)
        weights = jnp.exp(scores)
        weights = (weights / jnp.sum(weights, axis=-1, keepdims=True)).astype(jnp.bfloat16)
        blended = jnp.einsum(
            "hrk,khd->rhd", weights, value_block, preferred_element_type=jnp.float32
        ).astype(jnp.bfloat16)
        blended = blended.reshape(rows_dev, columns).astype(jnp.float32)
        blended = jnp.where(row_live[:, None], blended, jnp.zeros_like(blended))
        summed = summed.at[target].add(blended)
    attended = summed.astype(jnp.bfloat16)
    all_heads = lax.all_gather(attended, "head", axis=1, tiled=True)
    result = add_rows(all_heads, lax.all_gather(w_output, "ctx", axis=0, tiled=True))
    return result.astype(jnp.bfloat16)


def pairs(planes, move):
    found = []
    for z in range(planes):
        for x in range(2):
            for h in range(4):
                to = move(z, x, h)
                found.append(((2 * z + x) * 4 + h, (2 * to[0] + to[1]) * 4 + to[2]))
    return found


ACROSS_X = pairs(4, lambda z, x, h: (z, 1 - x, h))
ACROSS_Y = pairs(4, lambda z, x, h: (z, x, h ^ 2))
ACROSS_CORE = pairs(4, lambda z, x, h: (z, x, h ^ 1))
ONE_ALONG = pairs(4, lambda z, x, h: (z ^ 1, x, h))
TWO_ALONG = pairs(4, lambda z, x, h: (z ^ 2, x, h))
MID_TO_END = [pair for pair in ONE_ALONG if pair[0] // 8 in (1, 2)]
MID_TO_MID = pairs(4, lambda z, x, h: (3 - z if z in (1, 2) else z, x, h))
SAME_X = [[0, 2, 4, 6], [1, 3, 5, 7]]


def send(value, move):
    return lax.ppermute(value, AXES, move)


def along_z(value):
    return lax.all_gather(value, "ctx", axis=0, axis_index_groups=SAME_X)


def diagonal(groups):
    shape = (groups * 128, 128)
    row = lax.broadcasted_iota(jnp.int32, shape, 0) % 128
    return row == lax.broadcasted_iota(jnp.int32, shape, 1)


def pack(value, packed):
    rows, columns = value.shape
    groups = rows // 128
    peak = jnp.max(jnp.abs(value), axis=1, keepdims=True)
    power = jnp.clip(jnp.floor(jnp.log2(jnp.maximum(peak, 1e-30))) + 1.0, -90.0, 120.0)
    scaled = jnp.clip(jnp.round(value * jnp.exp2(15.0 - power)), -32767.0, 32767.0)
    packed[:rows, :] = scaled.astype(jnp.int32).astype(jnp.int16)
    spread = jnp.where(diagonal(groups), power, 0.0).reshape(groups, 128, 128).sum(axis=1)
    spread = jnp.concatenate([spread, jnp.zeros((16 - groups, 128), jnp.float32)], axis=0)
    packed[rows:, :128] = spread.astype(jnp.int32).astype(jnp.int16)
    packed[rows:, 128:] = jnp.zeros((16, columns - 128), jnp.int16)


def row_scale(packed):
    groups = (packed.shape[0] - 16) // 128
    spread = packed[groups * 128 :, :128].astype(jnp.int32).astype(jnp.float32)[:groups]
    spread = jnp.broadcast_to(spread[:, None, :], (groups, 128, 128)).reshape(groups * 128, 128)
    power = jnp.sum(jnp.where(diagonal(groups), spread, 0.0), axis=1, keepdims=True)
    return jnp.exp2(power - 15.0)


def unpack(packed, scale):
    return packed[: packed.shape[0] - 16, :].astype(jnp.int32).astype(jnp.float32) * scale


def query_body(place, *refs):
    own, near, (keep_weights, send_weights, kept, sent) = refs[:4], refs[4:8], refs[8:]

    def write(lefts):
        for weights, result in ((send_weights, sent), (keep_weights, kept)):
            total = None
            for j in range(4):
                term = jnp.dot(
                    lefts[j][...], weights[place[6 + j]], preferred_element_type=jnp.float32
                )
                total = term if total is None else total + term
            result[...] = total

    first_group = pl.program_id(0) < pl.num_programs(0) // 2
    pl.when(first_group)(lambda: write(own))
    pl.when(jnp.logical_not(first_group))(lambda: write(near))


def query_product(place, video_rows, near, weights):
    rows = video_rows.shape[0]
    depth, columns = weights.shape[1:]
    step = rows // 2
    half = columns // 2
    own_specs = [
        pl.BlockSpec(
            (step, depth),
            functools.partial(lambda j, i, place: (jnp.minimum(i, 1), place[j]), j),
        )
        for j in range(4)
    ]
    near_specs = [
        pl.BlockSpec(
            (step, depth), functools.partial(lambda j, i, place: (jnp.maximum(i - 2, 0), j % 2), j)
        )
        for j in range(4)
    ]
    part = jax.ShapeDtypeStruct((2 * rows, half), jnp.float32)
    return pl.pallas_call(
        query_body,
        grid_spec=pltpu.PrefetchScalarGridSpec(
            num_scalar_prefetch=1,
            grid=(4,),
            in_specs=own_specs
            + near_specs
            + [
                pl.BlockSpec((4, depth, half), lambda i, place: (0, 0, place[4])),
                pl.BlockSpec((4, depth, half), lambda i, place: (0, 0, place[5])),
            ],
            out_specs=[pl.BlockSpec((step, half), lambda i, place: (i, 0))] * 2,
        ),
        out_shape=[part, part],
        cost_estimate=pl.CostEstimate(
            flops=16 * rows * depth * columns,
            transcendentals=0,
            bytes_accessed=8 * (2 * rows + columns) * depth + 8 * rows * columns,
        ),
        name="query_product",
    )(place, *([video_rows] * 4), near[0], near[0], near[1], near[1], weights, weights)


def out_body(place, *refs, k_sizes):
    *lefts, weights, kept, sent = refs
    total = None
    for j in range(4):
        first = 0
        for i, size in enumerate(k_sizes):
            right = weights[place[j], first : first + size, :]
            term = jnp.dot(lefts[i * 4 + j][...], right, preferred_element_type=jnp.float32)
            total = term if total is None else total + term
            first += size
    pl.when(pl.program_id(0) < 2)(lambda: pack(total, sent))
    pl.when(pl.program_id(0) >= 2)(lambda: kept.__setitem__(..., total))


def out_product(place, groups, weights):
    rows = groups[0][0].shape[0]
    k_sizes = tuple(group[0].shape[1] for group in groups)
    columns = weights.shape[2]
    step = rows // 4
    left_specs = [
        pl.BlockSpec(
            (step, size), functools.partial(lambda skip, i, place: ((i + 2) % 4 + skip, 0), skip)
        )
        for size in k_sizes
        for skip in (0, 0, 0, 4)
    ]
    lefts = [piece for own, core, over_y in groups for piece in (own, core, over_y, core)]
    return pl.pallas_call(
        functools.partial(out_body, k_sizes=k_sizes),
        grid_spec=pltpu.PrefetchScalarGridSpec(
            num_scalar_prefetch=1,
            grid=(4,),
            in_specs=left_specs + [pl.BlockSpec(weights.shape, lambda i, place: (0, 0, 0))],
            out_specs=[
                pl.BlockSpec((step, columns), lambda i, place: (jnp.maximum(i - 2, 0), 0)),
                pl.BlockSpec((step + 16, columns), lambda i, place: (jnp.minimum(i, 1), 0)),
            ],
        ),
        out_shape=[
            jax.ShapeDtypeStruct((rows // 2, columns), jnp.float32),
            jax.ShapeDtypeStruct((2 * (step + 16), columns), jnp.int16),
        ],
        cost_estimate=pl.CostEstimate(
            flops=8 * rows * sum(k_sizes) * columns,
            transcendentals=0,
            bytes_accessed=8 * (rows + columns) * sum(k_sizes) + 4 * rows * columns,
        ),
        name="out_product",
    )(place, *lefts, weights)


def attend_body(kept, received, keys, values, speaker, attended, *, audio_length, heads):
    scale = 1.0 / HD**0.5
    of_row = speaker[...]
    lane = lax.broadcasted_iota(jnp.int32, (kept.shape[0], SPK * audio_length), 1)
    of_key = jnp.where(lane < audio_length, 1, 2)
    own_key = of_key == of_row
    live = of_row > 0
    for head in range(heads):
        at = slice(head * HD, (head + 1) * HD)
        query = (kept[:, at] + received[:, at]).astype(jnp.bfloat16)
        scores = (
            lax.dot_general(
                query, keys[:, at], (((1,), (1,)), ((), ())), preferred_element_type=jnp.float32
            )
            * scale
        )
        scores = jnp.where(own_key, scores, -1e30)
        scores = scores - jnp.max(scores, axis=-1, keepdims=True)
        weights = jnp.exp(scores)
        weights = (weights / jnp.sum(weights, axis=-1, keepdims=True)).astype(jnp.bfloat16)
        blended = jnp.dot(weights, values[:, at], preferred_element_type=jnp.float32)
        attended[:, at] = jnp.where(live, blended, 0.0).astype(jnp.bfloat16)


def attend(kept, received, keys, values, speaker, audio_length):
    rows, columns = kept.shape
    step = rows // 4
    at = lambda i: (i, 0)
    whole = pl.BlockSpec(keys.shape, lambda i: (0, 0))
    return pl.pallas_call(
        functools.partial(attend_body, audio_length=audio_length, heads=columns // HD),
        grid=(4,),
        in_specs=[
            pl.BlockSpec((step, columns), at),
            pl.BlockSpec((step, columns), lambda i: ((i + 2) % 4, 0)),
            whole,
            whole,
            pl.BlockSpec((step, 1), at),
        ],
        out_specs=pl.BlockSpec((step, columns), at),
        out_shape=jax.ShapeDtypeStruct((rows, columns), jnp.bfloat16),
        cost_estimate=pl.CostEstimate(
            flops=4 * rows * columns * SPK * audio_length,
            transcendentals=rows * SPK * audio_length * columns // HD,
            bytes_accessed=10 * rows * columns,
        ),
        name="attend",
    )(kept, received, keys, values, speaker)


def finish_body(kept, received, scales, *refs):
    refs[-1][...] = (kept[...] + unpack(received, row_scale(scales))).astype(
        jnp.bfloat16
    )


def finish(kept, received, first, whole, result):
    rows, columns = kept.shape
    step = rows // 2
    width = 2 * HD
    at = lambda i, j: (i, j)
    given = [] if result is None else [result]
    return pl.pallas_call(
        finish_body,
        grid=(2, columns // width),
        in_specs=[
            pl.BlockSpec((step, width), at),
            pl.BlockSpec((step + 16, width), at),
            pl.BlockSpec((step + 16, 128), lambda i, j: (i, 0)),
        ]
        + [pl.BlockSpec(memory_space=pl.ANY)] * len(given),
        out_specs=pl.BlockSpec((step, width), lambda i, j: (i, first // width + j)),
        out_shape=jax.ShapeDtypeStruct((rows, whole), jnp.bfloat16),
        input_output_aliases={3: 0} if given else {},
        cost_estimate=pl.CostEstimate(
            flops=2 * rows * columns, transcendentals=0, bytes_accessed=8 * rows * columns
        ),
        name="finish",
    )(kept, received, received, *given)


def head_pieces(value):
    over_y = send(value, ACROSS_Y)
    return value, send(jnp.concatenate([value, over_y], axis=0), ACROSS_CORE), over_y


def plane_shards(video_rows, w_query, w_output, audio_tokens, w_key, w_value, row_lists, row_counts):
    rows = video_rows.shape[0]
    block = w_query.shape[0]
    audio_width = audio_tokens.shape[2]
    ctx = lax.axis_index("ctx").astype(jnp.int32)
    h = lax.axis_index("head").astype(jnp.int32)
    x = ctx % 2
    core = h % 2

    z = ctx // 2
    is_mid = (z == 1) | (z == 2)

    def of_blocks(value, first, last):
        first, last = first * HD, last * HD
        return jnp.concatenate(
            [value[:, first:last], value[:, block + first : block + last]], axis=1
        )

    heads_block = block // HD
    gathered_weights = along_z(of_blocks(w_query, 0, GATHERED_HEADS))
    piece = of_blocks(w_query, GATHERED_HEADS, heads_block)
    swapped = send(piece, ONE_ALONG)
    opposite = send(piece, MID_TO_MID)
    last = send(swapped, MID_TO_MID)
    to_end = send(opposite, MID_TO_END)
    last_to_end = send(last, MID_TO_END)
    hopped_weights = jnp.stack(
        [
            piece,
            swapped,
            jnp.where(is_mid, last, to_end),
            jnp.where(is_mid, opposite, last_to_end),
        ]
    )

    near_block = lambda plane: lax.dynamic_slice(
        video_rows, (0, (2 * plane + 1 - x) * block), (rows, block)
    )
    near_half = send(
        jnp.concatenate([near_block(2 * core), near_block(2 * core + 1)], axis=1), ACROSS_X
    )
    near = [near_half, send(near_half, ACROSS_CORE)]
    planes = jnp.arange(4, dtype=jnp.int32)
    by_core = planes ^ (2 * core)
    place = jnp.concatenate([2 * by_core + x, jnp.stack([x, 1 - x])])

    position = jnp.arange(rows, dtype=jnp.int32)
    named = (row_lists[:, :, None] == position[None, None, :]) & (
        position[None, :, None] < row_counts[:, :, None]
    )
    speaker_of = jnp.sum(
        jnp.any(named, axis=1) * jnp.array([[1], [2]], jnp.int32), axis=0
    ).astype(jnp.bfloat16)
    tokens = audio_tokens.shape[1]
    gathered = jnp.concatenate([audio_tokens.reshape(-1), speaker_of])[None]
    for move in (ACROSS_X, ONE_ALONG, TWO_ALONG):
        gathered = jnp.concatenate([gathered, send(gathered, move)], axis=0)
    whole_audio = (
        gathered[:, : SPK * tokens * audio_width]
        .reshape(-1, SPK, tokens, audio_width)
        .transpose(1, 0, 2, 3)
        .reshape(-1, audio_width)
    )
    audio_length = whole_audio.shape[0] // SPK
    speakers = gathered[:2, SPK * tokens * audio_width :].astype(jnp.int32)
    own_block = lambda weights: lax.dynamic_slice(weights, (0, x * block), (audio_width, block))
    key_rows = add_rows(whole_audio, own_block(w_key)).astype(jnp.bfloat16)
    value_rows = add_rows(whole_audio, own_block(w_value)).astype(jnp.bfloat16)

    speaker = speakers.reshape(-1, 1)
    attended = []
    for weights, order, first, last in (
        (gathered_weights, by_core, 0, GATHERED_HEADS),
        (hopped_weights, by_core ^ z, GATHERED_HEADS, heads_block),
    ):
        at = slice(first * HD, last * HD)
        kept, sent = query_product(
            jnp.concatenate([place, order]), video_rows, near, weights
        )
        attended.append(
            head_pieces(
                attend(
                    kept,
                    send(sent, ACROSS_X),
                    key_rows[:, at],
                    value_rows[:, at],
                    speaker,
                    audio_length,
                )
            )
        )

    result = None
    first = 0
    for heads in OUT_CHUNKS:
        size = heads * HD
        weights = along_z(w_output[:, first : first + size])
        kept, sent = out_product(planes ^ h, attended, weights)
        result = finish(kept, send(sent, ACROSS_X), first, w_output.shape[1], result)
        first += size
    return result


def solution(mesh):
    in_specs = (
        P("ctx", None),
        P("ctx", "head"),
        P("ctx", "head"),
        P(None, "ctx", None),
        P(None, "head"),
        P(None, "head"),
        P(None, "ctx"),
        P(None, "ctx"),
    )
    out_specs = P("ctx", "head")
    planes = mesh.shape["ctx"] == 8 and mesh.shape["head"] == 4
    shards = plane_shards if planes else plain_shards
    return jax.shard_map(shards, mesh=mesh, in_specs=in_specs, out_specs=out_specs, check_vma=False)
```

```python
import functools

import jax
import jax.numpy as jnp
from jax import lax
from jax.experimental import pallas as pl
from jax.experimental.pallas import tpu as pltpu
from jax.sharding import PartitionSpec as P

HD = 128
SPK = 2
AXES = ("ctx", "head")
GATHERED_HEADS = 3
OUT_CHUNKS = (8, 2)


def add_rows(left_rows, shard_piece):
    return jnp.dot(left_rows, shard_piece, preferred_element_type=jnp.float32)


def plain_shards(video_rows, w_query, w_output, audio_tokens, w_key, w_value, row_lists, row_counts):
    rows_dev = video_rows.shape[0]
    columns = w_query.shape[1]
    heads_dev = columns // HD
    queries = add_rows(video_rows, lax.all_gather(w_query, "ctx", axis=0, tiled=True)).astype(
        jnp.bfloat16
    )
    whole_audio = lax.all_gather(audio_tokens, "ctx", axis=1, tiled=True)
    key_rows = jnp.einsum(
        "sta,ad->std", whole_audio, w_key, preferred_element_type=jnp.float32
    ).astype(jnp.bfloat16)
    value_rows = jnp.einsum(
        "sta,ad->std", whole_audio, w_value, preferred_element_type=jnp.float32
    ).astype(jnp.bfloat16)
    audio_length = key_rows.shape[1]
    position = jnp.arange(rows_dev, dtype=jnp.int32)
    score_scale = 1.0 / HD**0.5
    summed = jnp.zeros((rows_dev, columns), jnp.float32)
    for speaker in range(SPK):
        target = row_lists[speaker]
        row_live = position < row_counts[speaker, 0]
        picked = queries[target].reshape(rows_dev, heads_dev, HD)
        key_block = key_rows[speaker].reshape(audio_length, heads_dev, HD)
        value_block = value_rows[speaker].reshape(audio_length, heads_dev, HD)
        scores = (
            jnp.einsum("rhd,khd->hrk", picked, key_block, preferred_element_type=jnp.float32)
            * score_scale
        )
        scores = scores - jnp.max(scores, axis=-1, keepdims=True)
        weights = jnp.exp(scores)
        weights = (weights / jnp.sum(weights, axis=-1, keepdims=True)).astype(jnp.bfloat16)
        blended = jnp.einsum(
            "hrk,khd->rhd", weights, value_block, preferred_element_type=jnp.float32
        ).astype(jnp.bfloat16)
        blended = blended.reshape(rows_dev, columns).astype(jnp.float32)
        blended = jnp.where(row_live[:, None], blended, jnp.zeros_like(blended))
        summed = summed.at[target].add(blended)
    attended = summed.astype(jnp.bfloat16)
    all_heads = lax.all_gather(attended, "head", axis=1, tiled=True)
    result = add_rows(all_heads, lax.all_gather(w_output, "ctx", axis=0, tiled=True))
    return result.astype(jnp.bfloat16)


def pairs(planes, move):
    found = []
    for z in range(planes):
        for x in range(2):
            for h in range(4):
                to = move(z, x, h)
                found.append(((2 * z + x) * 4 + h, (2 * to[0] + to[1]) * 4 + to[2]))
    return found


ACROSS_X = pairs(4, lambda z, x, h: (z, 1 - x, h))
ACROSS_Y = pairs(4, lambda z, x, h: (z, x, h ^ 2))
ACROSS_CORE = pairs(4, lambda z, x, h: (z, x, h ^ 1))
ONE_ALONG = pairs(4, lambda z, x, h: (z ^ 1, x, h))
TWO_ALONG = pairs(4, lambda z, x, h: (z ^ 2, x, h))
MID_TO_END = [pair for pair in ONE_ALONG if pair[0] // 8 in (1, 2)]
MID_TO_MID = pairs(4, lambda z, x, h: (3 - z if z in (1, 2) else z, x, h))
SAME_X = [[0, 2, 4, 6], [1, 3, 5, 7]]


def send(value, move):
    return lax.ppermute(value, AXES, move)


def along_z(value):
    return lax.all_gather(value, "ctx", axis=0, axis_index_groups=SAME_X)


def diagonal(groups):
    shape = (groups * 128, 128)
    row = lax.broadcasted_iota(jnp.int32, shape, 0) % 128
    return row == lax.broadcasted_iota(jnp.int32, shape, 1)


def pack(value, packed):
    rows, columns = value.shape
    groups = rows // 128
    peak = jnp.max(jnp.abs(value), axis=1, keepdims=True)
    power = jnp.clip(jnp.floor(jnp.log2(jnp.maximum(peak, 1e-30))) + 1.0, -90.0, 120.0)
    scaled = jnp.clip(jnp.round(value * jnp.exp2(15.0 - power)), -32767.0, 32767.0)
    packed[:rows, :] = scaled.astype(jnp.int32).astype(jnp.int16)
    spread = jnp.where(diagonal(groups), power, 0.0).reshape(groups, 128, 128).sum(axis=1)
    spread = jnp.concatenate([spread, jnp.zeros((16 - groups, 128), jnp.float32)], axis=0)
    packed[rows:, :128] = spread.astype(jnp.int32).astype(jnp.int16)
    packed[rows:, 128:] = jnp.zeros((16, columns - 128), jnp.int16)


def row_scale(packed):
    groups = (packed.shape[0] - 16) // 128
    spread = packed[groups * 128 :, :128].astype(jnp.int32).astype(jnp.float32)[:groups]
    spread = jnp.broadcast_to(spread[:, None, :], (groups, 128, 128)).reshape(groups * 128, 128)
    power = jnp.sum(jnp.where(diagonal(groups), spread, 0.0), axis=1, keepdims=True)
    return jnp.exp2(power - 15.0)


def unpack(packed, scale):
    return packed[: packed.shape[0] - 16, :].astype(jnp.int32).astype(jnp.float32) * scale


def query_body(place, *refs):
    own, near, (keep_weights, send_weights, kept, sent) = refs[:4], refs[4:8], refs[8:]

    def write(lefts):
        for weights, result in ((send_weights, sent), (keep_weights, kept)):
            total = None
            for j in range(4):
                term = jnp.dot(
                    lefts[j][...], weights[place[6 + j]], preferred_element_type=jnp.float32
                )
                total = term if total is None else total + term
            result[...] = total

    first_group = pl.program_id(0) < pl.num_programs(0) // 2
    pl.when(first_group)(lambda: write(own))
    pl.when(jnp.logical_not(first_group))(lambda: write(near))


def query_product(place, video_rows, near, weights):
    rows = video_rows.shape[0]
    depth, columns = weights.shape[1:]
    step = rows // 2
    half = columns // 2
    own_specs = [
        pl.BlockSpec(
            (step, depth),
            functools.partial(lambda j, i, place: (jnp.minimum(i, 1), place[j]), j),
        )
        for j in range(4)
    ]
    near_specs = [
        pl.BlockSpec(
            (step, depth), functools.partial(lambda j, i, place: (jnp.maximum(i - 2, 0), j % 2), j)
        )
        for j in range(4)
    ]
    part = jax.ShapeDtypeStruct((2 * rows, half), jnp.float32)
    return pl.pallas_call(
        query_body,
        grid_spec=pltpu.PrefetchScalarGridSpec(
            num_scalar_prefetch=1,
            grid=(4,),
            in_specs=own_specs
            + near_specs
            + [
                pl.BlockSpec((4, depth, half), lambda i, place: (0, 0, place[4])),
                pl.BlockSpec((4, depth, half), lambda i, place: (0, 0, place[5])),
            ],
            out_specs=[pl.BlockSpec((step, half), lambda i, place: (i, 0))] * 2,
        ),
        out_shape=[part, part],
        cost_estimate=pl.CostEstimate(
            flops=16 * rows * depth * columns,
            transcendentals=0,
            bytes_accessed=8 * (2 * rows + columns) * depth + 8 * rows * columns,
        ),
        name="query_product",
    )(place, *([video_rows] * 4), near[0], near[0], near[1], near[1], weights, weights)


def out_body(place, *refs, k_sizes):
    *lefts, weights, kept, sent = refs
    total = None
    for j in range(4):
        first = 0
        for i, size in enumerate(k_sizes):
            right = weights[place[j], first : first + size, :]
            term = jnp.dot(lefts[i * 4 + j][...], right, preferred_element_type=jnp.float32)
            total = term if total is None else total + term
            first += size
    pl.when(pl.program_id(0) == 0)(lambda: pack(total, sent))
    pl.when(pl.program_id(0) == 1)(lambda: kept.__setitem__(..., total))


def out_product(place, groups, weights):
    rows = groups[0][0].shape[0]
    k_sizes = tuple(group[0].shape[1] for group in groups)
    columns = weights.shape[2]
    step = rows // 2
    left_specs = [
        pl.BlockSpec(
            (step, size), functools.partial(lambda skip, i, place: (1 - i + skip, 0), skip)
        )
        for size in k_sizes
        for skip in (0, 0, 0, 2)
    ]
    lefts = [piece for own, core, over_y in groups for piece in (own, core, over_y, core)]
    return pl.pallas_call(
        functools.partial(out_body, k_sizes=k_sizes),
        grid_spec=pltpu.PrefetchScalarGridSpec(
            num_scalar_prefetch=1,
            grid=(2,),
            in_specs=left_specs + [pl.BlockSpec(weights.shape, lambda i, place: (0, 0, 0))],
            out_specs=[
                pl.BlockSpec((step, columns), lambda i, place: (0, 0)),
                pl.BlockSpec((step + 16, columns), lambda i, place: (0, 0)),
            ],
        ),
        out_shape=[
            jax.ShapeDtypeStruct((step, columns), jnp.float32),
            jax.ShapeDtypeStruct((step + 16, columns), jnp.int16),
        ],
        cost_estimate=pl.CostEstimate(
            flops=8 * rows * sum(k_sizes) * columns,
            transcendentals=0,
            bytes_accessed=8 * (rows + columns) * sum(k_sizes) + 4 * rows * columns,
        ),
        name="out_product",
    )(place, *lefts, weights)


def attend_body(kept, received, keys, values, speaker, attended, *, audio_length, heads):
    scale = 1.0 / HD**0.5
    of_row = speaker[...]
    lane = lax.broadcasted_iota(jnp.int32, (kept.shape[0], SPK * audio_length), 1)
    of_key = jnp.where(lane < audio_length, 1, 2)
    own_key = of_key == of_row
    live = of_row > 0
    for head in range(heads):
        at = slice(head * HD, (head + 1) * HD)
        query = (kept[:, at] + received[:, at]).astype(jnp.bfloat16)
        scores = (
            lax.dot_general(
                query, keys[:, at], (((1,), (1,)), ((), ())), preferred_element_type=jnp.float32
            )
            * scale
        )
        scores = jnp.where(own_key, scores, -1e30)
        scores = scores - jnp.max(scores, axis=-1, keepdims=True)
        weights = jnp.exp(scores)
        weights = (weights / jnp.sum(weights, axis=-1, keepdims=True)).astype(jnp.bfloat16)
        blended = jnp.dot(weights, values[:, at], preferred_element_type=jnp.float32)
        attended[:, at] = jnp.where(live, blended, 0.0).astype(jnp.bfloat16)


def attend(kept, received, keys, values, speaker, audio_length):
    rows, columns = kept.shape
    step = rows // 4
    at = lambda i: (i, 0)
    whole = pl.BlockSpec(keys.shape, lambda i: (0, 0))
    return pl.pallas_call(
        functools.partial(attend_body, audio_length=audio_length, heads=columns // HD),
        grid=(4,),
        in_specs=[
            pl.BlockSpec((step, columns), at),
            pl.BlockSpec((step, columns), lambda i: ((i + 2) % 4, 0)),
            whole,
            whole,
            pl.BlockSpec((step, 1), at),
        ],
        out_specs=pl.BlockSpec((step, columns), at),
        out_shape=jax.ShapeDtypeStruct((rows, columns), jnp.bfloat16),
        cost_estimate=pl.CostEstimate(
            flops=4 * rows * columns * SPK * audio_length,
            transcendentals=rows * SPK * audio_length * columns // HD,
            bytes_accessed=10 * rows * columns,
        ),
        name="attend",
    )(kept, received, keys, values, speaker)


def finish_body(kept, received, scales, *refs):
    refs[-1][...] = (kept[...] + unpack(received, row_scale(scales))).astype(
        jnp.bfloat16
    )


def finish(kept, received, first, whole, result):
    rows, columns = kept.shape
    width = 4 * HD if columns % (4 * HD) == 0 and first % (4 * HD) == 0 else 2 * HD
    at = lambda j: (0, j)
    given = [] if result is None else [result]
    return pl.pallas_call(
        finish_body,
        grid=(columns // width,),
        in_specs=[
            pl.BlockSpec((rows, width), at),
            pl.BlockSpec((rows + 16, width), at),
            pl.BlockSpec((rows + 16, 128), lambda j: (0, 0)),
        ]
        + [pl.BlockSpec(memory_space=pl.ANY)] * len(given),
        out_specs=pl.BlockSpec((rows, width), lambda j: (0, first // width + j)),
        out_shape=jax.ShapeDtypeStruct((rows, whole), jnp.bfloat16),
        input_output_aliases={3: 0} if given else {},
        cost_estimate=pl.CostEstimate(
            flops=2 * rows * columns, transcendentals=0, bytes_accessed=8 * rows * columns
        ),
        name="finish",
    )(kept, received, received, *given)


def head_pieces(value):
    over_y = send(value, ACROSS_Y)
    return value, send(jnp.concatenate([value, over_y], axis=0), ACROSS_CORE), over_y


def plane_shards(video_rows, w_query, w_output, audio_tokens, w_key, w_value, row_lists, row_counts):
    rows = video_rows.shape[0]
    block = w_query.shape[0]
    audio_width = audio_tokens.shape[2]
    ctx = lax.axis_index("ctx").astype(jnp.int32)
    h = lax.axis_index("head").astype(jnp.int32)
    x = ctx % 2
    core = h % 2

    z = ctx // 2
    is_mid = (z == 1) | (z == 2)

    def of_blocks(value, first, last):
        first, last = first * HD, last * HD
        return jnp.concatenate(
            [value[:, first:last], value[:, block + first : block + last]], axis=1
        )

    heads_block = block // HD
    gathered_weights = along_z(of_blocks(w_query, 0, GATHERED_HEADS))
    piece = of_blocks(w_query, GATHERED_HEADS, heads_block)
    swapped = send(piece, ONE_ALONG)
    opposite = send(piece, MID_TO_MID)
    last = send(swapped, MID_TO_MID)
    to_end = send(opposite, MID_TO_END)
    last_to_end = send(last, MID_TO_END)
    hopped_weights = jnp.stack(
        [
            piece,
            swapped,
            jnp.where(is_mid, last, to_end),
            jnp.where(is_mid, opposite, last_to_end),
        ]
    )

    near_block = lambda plane: lax.dynamic_slice(
        video_rows, (0, (2 * plane + 1 - x) * block), (rows, block)
    )
    near_half = send(
        jnp.concatenate([near_block(2 * core), near_block(2 * core + 1)], axis=1), ACROSS_X
    )
    near = [near_half, send(near_half, ACROSS_CORE)]
    planes = jnp.arange(4, dtype=jnp.int32)
    by_core = planes ^ (2 * core)
    place = jnp.concatenate([2 * by_core + x, jnp.stack([x, 1 - x])])

    position = jnp.arange(rows, dtype=jnp.int32)
    named = (row_lists[:, :, None] == position[None, None, :]) & (
        position[None, :, None] < row_counts[:, :, None]
    )
    speaker_of = jnp.sum(
        jnp.any(named, axis=1) * jnp.array([[1], [2]], jnp.int32), axis=0
    ).astype(jnp.bfloat16)
    tokens = audio_tokens.shape[1]
    gathered = jnp.concatenate([audio_tokens.reshape(-1), speaker_of])[None]
    for move in (ACROSS_X, ONE_ALONG, TWO_ALONG):
        gathered = jnp.concatenate([gathered, send(gathered, move)], axis=0)
    whole_audio = (
        gathered[:, : SPK * tokens * audio_width]
        .reshape(-1, SPK, tokens, audio_width)
        .transpose(1, 0, 2, 3)
        .reshape(-1, audio_width)
    )
    audio_length = whole_audio.shape[0] // SPK
    speakers = gathered[:2, SPK * tokens * audio_width :].astype(jnp.int32)
    own_block = lambda weights: lax.dynamic_slice(weights, (0, x * block), (audio_width, block))
    key_rows = add_rows(whole_audio, own_block(w_key)).astype(jnp.bfloat16)
    value_rows = add_rows(whole_audio, own_block(w_value)).astype(jnp.bfloat16)

    speaker = speakers.reshape(-1, 1)
    attended = []
    for weights, order, first, last in (
        (gathered_weights, by_core, 0, GATHERED_HEADS),
        (hopped_weights, by_core ^ z, GATHERED_HEADS, heads_block),
    ):
        at = slice(first * HD, last * HD)
        kept, sent = query_product(
            jnp.concatenate([place, order]), video_rows, near, weights
        )
        attended.append(
            head_pieces(
                attend(
                    kept,
                    send(sent, ACROSS_X),
                    key_rows[:, at],
                    value_rows[:, at],
                    speaker,
                    audio_length,
                )
            )
        )

    result = None
    first = 0
    for heads in OUT_CHUNKS:
        size = heads * HD
        weights = along_z(w_output[:, first : first + size])
        kept, sent = out_product(planes ^ h, attended, weights)
        result = finish(kept, send(sent, ACROSS_X), first, w_output.shape[1], result)
        first += size
    return result


def solution(mesh):
    in_specs = (
        P("ctx", None),
        P("ctx", "head"),
        P("ctx", "head"),
        P(None, "ctx", None),
        P(None, "head"),
        P(None, "head"),
        P(None, "ctx"),
        P(None, "ctx"),
    )
    out_specs = P("ctx", "head")
    planes = mesh.shape["ctx"] == 8 and mesh.shape["head"] == 4
    shards = plane_shards if planes else plain_shards
    return jax.shard_map(shards, mesh=mesh, in_specs=in_specs, out_specs=out_specs, check_vma=False)
```

```python
import functools

import jax
import jax.numpy as jnp
from jax import lax
from jax.experimental import pallas as pl
from jax.experimental.pallas import tpu as pltpu
from jax.sharding import PartitionSpec as P

HD = 128
SPK = 2
AXES = ("ctx", "head")
GATHERED_HEADS = 3
OUT_CHUNKS = (8, 2)


def add_rows(left_rows, shard_piece):
    return jnp.dot(left_rows, shard_piece, preferred_element_type=jnp.float32)


def plain_shards(video_rows, w_query, w_output, audio_tokens, w_key, w_value, row_lists, row_counts):
    rows_dev = video_rows.shape[0]
    columns = w_query.shape[1]
    heads_dev = columns // HD
    queries = add_rows(video_rows, lax.all_gather(w_query, "ctx", axis=0, tiled=True)).astype(
        jnp.bfloat16
    )
    whole_audio = lax.all_gather(audio_tokens, "ctx", axis=1, tiled=True)
    key_rows = jnp.einsum(
        "sta,ad->std", whole_audio, w_key, preferred_element_type=jnp.float32
    ).astype(jnp.bfloat16)
    value_rows = jnp.einsum(
        "sta,ad->std", whole_audio, w_value, preferred_element_type=jnp.float32
    ).astype(jnp.bfloat16)
    audio_length = key_rows.shape[1]
    position = jnp.arange(rows_dev, dtype=jnp.int32)
    score_scale = 1.0 / HD**0.5
    summed = jnp.zeros((rows_dev, columns), jnp.float32)
    for speaker in range(SPK):
        target = row_lists[speaker]
        row_live = position < row_counts[speaker, 0]
        picked = queries[target].reshape(rows_dev, heads_dev, HD)
        key_block = key_rows[speaker].reshape(audio_length, heads_dev, HD)
        value_block = value_rows[speaker].reshape(audio_length, heads_dev, HD)
        scores = (
            jnp.einsum("rhd,khd->hrk", picked, key_block, preferred_element_type=jnp.float32)
            * score_scale
        )
        scores = scores - jnp.max(scores, axis=-1, keepdims=True)
        weights = jnp.exp(scores)
        weights = (weights / jnp.sum(weights, axis=-1, keepdims=True)).astype(jnp.bfloat16)
        blended = jnp.einsum(
            "hrk,khd->rhd", weights, value_block, preferred_element_type=jnp.float32
        ).astype(jnp.bfloat16)
        blended = blended.reshape(rows_dev, columns).astype(jnp.float32)
        blended = jnp.where(row_live[:, None], blended, jnp.zeros_like(blended))
        summed = summed.at[target].add(blended)
    attended = summed.astype(jnp.bfloat16)
    all_heads = lax.all_gather(attended, "head", axis=1, tiled=True)
    result = add_rows(all_heads, lax.all_gather(w_output, "ctx", axis=0, tiled=True))
    return result.astype(jnp.bfloat16)


def pairs(planes, move):
    found = []
    for z in range(planes):
        for x in range(2):
            for h in range(4):
                to = move(z, x, h)
                found.append(((2 * z + x) * 4 + h, (2 * to[0] + to[1]) * 4 + to[2]))
    return found


ACROSS_X = pairs(4, lambda z, x, h: (z, 1 - x, h))
ACROSS_Y = pairs(4, lambda z, x, h: (z, x, h ^ 2))
ACROSS_CORE = pairs(4, lambda z, x, h: (z, x, h ^ 1))
ONE_ALONG = pairs(4, lambda z, x, h: (z ^ 1, x, h))
TWO_ALONG = pairs(4, lambda z, x, h: (z ^ 2, x, h))
MID_TO_END = [pair for pair in ONE_ALONG if pair[0] // 8 in (1, 2)]
MID_TO_MID = pairs(4, lambda z, x, h: (3 - z if z in (1, 2) else z, x, h))
SAME_X = [[0, 2, 4, 6], [1, 3, 5, 7]]


def send(value, move):
    return lax.ppermute(value, AXES, move)


def along_z(value):
    return lax.all_gather(value, "ctx", axis=0, axis_index_groups=SAME_X)


def diagonal(groups):
    shape = (groups * 128, 128)
    row = lax.broadcasted_iota(jnp.int32, shape, 0) % 128
    return row == lax.broadcasted_iota(jnp.int32, shape, 1)


def pack(value, packed):
    rows, columns = value.shape
    groups = rows // 128
    peak = jnp.max(jnp.abs(value), axis=1, keepdims=True)
    power = jnp.clip(jnp.floor(jnp.log2(jnp.maximum(peak, 1e-33))) + 1.0, -110.0, 120.0)
    scaled = jnp.clip(jnp.round(value * jnp.exp2(15.0 - power)), -32767.0, 32767.0)
    packed[:rows, :] = scaled.astype(jnp.int32).astype(jnp.int16)
    spread = jnp.where(diagonal(groups), power, 0.0).reshape(groups, 128, 128).sum(axis=1)
    spread = jnp.concatenate([spread, jnp.zeros((16 - groups, 128), jnp.float32)], axis=0)
    packed[rows:, :128] = spread.astype(jnp.int32).astype(jnp.int16)
    packed[rows:, 128:] = jnp.zeros((16, columns - 128), jnp.int16)


def row_scale(packed):
    groups = (packed.shape[0] - 16) // 128
    spread = packed[groups * 128 :, :128].astype(jnp.int32).astype(jnp.float32)[:groups]
    spread = jnp.broadcast_to(spread[:, None, :], (groups, 128, 128)).reshape(groups * 128, 128)
    power = jnp.sum(jnp.where(diagonal(groups), spread, 0.0), axis=1, keepdims=True)
    return jnp.exp2(power - 15.0)


def unpack(packed, scale):
    return packed[: packed.shape[0] - 16, :].astype(jnp.int32).astype(jnp.float32) * scale


def query_body(place, *refs):
    own, near, (keep_weights, send_weights, kept, sent) = refs[:4], refs[4:8], refs[8:]

    def write(lefts):
        for weights, result in ((send_weights, sent), (keep_weights, kept)):
            total = None
            for j in range(4):
                term = jnp.dot(
                    lefts[j][...], weights[place[6 + j]], preferred_element_type=jnp.float32
                )
                total = term if total is None else total + term
            result[...] = total

    first_group = pl.program_id(0) < pl.num_programs(0) // 2
    pl.when(first_group)(lambda: write(own))
    pl.when(jnp.logical_not(first_group))(lambda: write(near))


def query_product(place, video_rows, near, weights):
    rows = video_rows.shape[0]
    depth, columns = weights.shape[1:]
    step = rows // 2
    half = columns // 2
    own_specs = [
        pl.BlockSpec(
            (step, depth),
            functools.partial(lambda j, i, place: (jnp.minimum(i, 1), place[j]), j),
        )
        for j in range(4)
    ]
    near_specs = [
        pl.BlockSpec(
            (step, depth), functools.partial(lambda j, i, place: (jnp.maximum(i - 2, 0), j % 2), j)
        )
        for j in range(4)
    ]
    part = jax.ShapeDtypeStruct((2 * rows, half), jnp.float32)
    return pl.pallas_call(
        query_body,
        grid_spec=pltpu.PrefetchScalarGridSpec(
            num_scalar_prefetch=1,
            grid=(4,),
            in_specs=own_specs
            + near_specs
            + [
                pl.BlockSpec((4, depth, half), lambda i, place: (0, 0, place[4])),
                pl.BlockSpec((4, depth, half), lambda i, place: (0, 0, place[5])),
            ],
            out_specs=[pl.BlockSpec((step, half), lambda i, place: (i, 0))] * 2,
        ),
        out_shape=[part, part],
        cost_estimate=pl.CostEstimate(
            flops=16 * rows * depth * columns,
            transcendentals=0,
            bytes_accessed=8 * (2 * rows + columns) * depth + 8 * rows * columns,
        ),
        name="query_product",
    )(place, *([video_rows] * 4), near[0], near[0], near[1], near[1], weights, weights)


def out_body(place, *refs, k_sizes):
    *lefts, weights, kept, sent = refs
    total = None
    for j in range(4):
        first = 0
        for i, size in enumerate(k_sizes):
            right = weights[place[j], first : first + size, :]
            term = jnp.dot(lefts[i * 4 + j][...], right, preferred_element_type=jnp.float32)
            total = term if total is None else total + term
            first += size
    pl.when(pl.program_id(0) == 0)(lambda: pack(total, sent))
    pl.when(pl.program_id(0) == 1)(lambda: kept.__setitem__(..., total))


def out_product(place, groups, weights):
    rows = groups[0][0].shape[0]
    k_sizes = tuple(group[0].shape[1] for group in groups)
    columns = weights.shape[2]
    step = rows // 2
    left_specs = [
        pl.BlockSpec(
            (step, size), functools.partial(lambda skip, i, place: (1 - i + skip, 0), skip)
        )
        for size in k_sizes
        for skip in (0, 0, 0, 2)
    ]
    lefts = [piece for own, core, over_y in groups for piece in (own, core, over_y, core)]
    return pl.pallas_call(
        functools.partial(out_body, k_sizes=k_sizes),
        grid_spec=pltpu.PrefetchScalarGridSpec(
            num_scalar_prefetch=1,
            grid=(2,),
            in_specs=left_specs + [pl.BlockSpec(weights.shape, lambda i, place: (0, 0, 0))],
            out_specs=[
                pl.BlockSpec((step, columns), lambda i, place: (0, 0)),
                pl.BlockSpec((step + 16, columns), lambda i, place: (0, 0)),
            ],
        ),
        out_shape=[
            jax.ShapeDtypeStruct((step, columns), jnp.float32),
            jax.ShapeDtypeStruct((step + 16, columns), jnp.int16),
        ],
        cost_estimate=pl.CostEstimate(
            flops=8 * rows * sum(k_sizes) * columns,
            transcendentals=0,
            bytes_accessed=8 * (rows + columns) * sum(k_sizes) + 4 * rows * columns,
        ),
        name="out_product",
    )(place, *lefts, weights)


def attend_body(kept, received, keys, values, speaker, attended, *, audio_length, heads):
    scale = 1.0 / HD**0.5
    of_row = speaker[...]
    lane = lax.broadcasted_iota(jnp.int32, (kept.shape[0], SPK * audio_length), 1)
    of_key = jnp.where(lane < audio_length, 1, 2)
    own_key = of_key == of_row
    live = of_row > 0
    for head in range(heads):
        at = slice(head * HD, (head + 1) * HD)
        query = (kept[:, at] + received[:, at]).astype(jnp.bfloat16)
        scores = (
            lax.dot_general(
                query, keys[:, at], (((1,), (1,)), ((), ())), preferred_element_type=jnp.float32
            )
            * scale
        )
        scores = jnp.where(own_key, scores, -1e30)
        scores = scores - jnp.max(scores, axis=-1, keepdims=True)
        weights = jnp.exp(scores)
        weights = (weights / jnp.sum(weights, axis=-1, keepdims=True)).astype(jnp.bfloat16)
        blended = jnp.dot(weights, values[:, at], preferred_element_type=jnp.float32)
        attended[:, at] = jnp.where(live, blended, 0.0).astype(jnp.bfloat16)


def attend(kept, received, keys, values, speaker, audio_length):
    rows, columns = kept.shape
    step = rows // 4
    at = lambda i: (i, 0)
    whole = pl.BlockSpec(keys.shape, lambda i: (0, 0))
    return pl.pallas_call(
        functools.partial(attend_body, audio_length=audio_length, heads=columns // HD),
        grid=(4,),
        in_specs=[
            pl.BlockSpec((step, columns), at),
            pl.BlockSpec((step, columns), lambda i: ((i + 2) % 4, 0)),
            whole,
            whole,
            pl.BlockSpec((step, 1), at),
        ],
        out_specs=pl.BlockSpec((step, columns), at),
        out_shape=jax.ShapeDtypeStruct((rows, columns), jnp.bfloat16),
        cost_estimate=pl.CostEstimate(
            flops=4 * rows * columns * SPK * audio_length,
            transcendentals=rows * SPK * audio_length * columns // HD,
            bytes_accessed=10 * rows * columns,
        ),
        name="attend",
    )(kept, received, keys, values, speaker)


def finish_body(kept, received, scales, *refs):
    refs[-1][...] = (kept[...] + unpack(received, row_scale(scales))).astype(
        jnp.bfloat16
    )


def finish(kept, received, first, whole, result):
    rows, columns = kept.shape
    width = 4 * HD if columns % (4 * HD) == 0 and first % (4 * HD) == 0 else 2 * HD
    at = lambda j: (0, j)
    given = [] if result is None else [result]
    return pl.pallas_call(
        finish_body,
        grid=(columns // width,),
        in_specs=[
            pl.BlockSpec((rows, width), at),
            pl.BlockSpec((rows + 16, width), at),
            pl.BlockSpec((rows + 16, 128), lambda j: (0, 0)),
        ]
        + [pl.BlockSpec(memory_space=pl.ANY)] * len(given),
        out_specs=pl.BlockSpec((rows, width), lambda j: (0, first // width + j)),
        out_shape=jax.ShapeDtypeStruct((rows, whole), jnp.bfloat16),
        input_output_aliases={3: 0} if given else {},
        cost_estimate=pl.CostEstimate(
            flops=2 * rows * columns, transcendentals=0, bytes_accessed=8 * rows * columns
        ),
        name="finish",
    )(kept, received, received, *given)


def head_pieces(value):
    over_y = send(value, ACROSS_Y)
    return value, send(jnp.concatenate([value, over_y], axis=0), ACROSS_CORE), over_y


def plane_shards(video_rows, w_query, w_output, audio_tokens, w_key, w_value, row_lists, row_counts):
    rows = video_rows.shape[0]
    block = w_query.shape[0]
    audio_width = audio_tokens.shape[2]
    ctx = lax.axis_index("ctx").astype(jnp.int32)
    h = lax.axis_index("head").astype(jnp.int32)
    x = ctx % 2
    core = h % 2

    z = ctx // 2
    is_mid = (z == 1) | (z == 2)

    def of_blocks(value, first, last):
        first, last = first * HD, last * HD
        return jnp.concatenate(
            [value[:, first:last], value[:, block + first : block + last]], axis=1
        )

    heads_block = block // HD
    gathered_weights = along_z(of_blocks(w_query, 0, GATHERED_HEADS))
    piece = of_blocks(w_query, GATHERED_HEADS, heads_block)
    swapped = send(piece, ONE_ALONG)
    opposite = send(piece, MID_TO_MID)
    last = send(swapped, MID_TO_MID)
    to_end = send(opposite, MID_TO_END)
    last_to_end = send(last, MID_TO_END)
    hopped_weights = jnp.stack(
        [
            piece,
            swapped,
            jnp.where(is_mid, last, to_end),
            jnp.where(is_mid, opposite, last_to_end),
        ]
    )

    near_block = lambda plane: lax.dynamic_slice(
        video_rows, (0, (2 * plane + 1 - x) * block), (rows, block)
    )
    near_half = jnp.concatenate([near_block(2 * core), near_block(2 * core + 1)], axis=1)
    near_half, piece = lax.optimization_barrier((near_half, piece))
    near_half = send(near_half, ACROSS_X)
    near = [near_half, send(near_half, ACROSS_CORE)]
    planes = jnp.arange(4, dtype=jnp.int32)
    by_core = planes ^ (2 * core)
    place = jnp.concatenate([2 * by_core + x, jnp.stack([x, 1 - x])])

    position = jnp.arange(rows, dtype=jnp.int32)
    named = (row_lists[:, :, None] == position[None, None, :]) & (
        position[None, :, None] < row_counts[:, :, None]
    )
    speaker_of = jnp.sum(
        jnp.any(named, axis=1) * jnp.array([[1], [2]], jnp.int32), axis=0
    ).astype(jnp.bfloat16)
    tokens = audio_tokens.shape[1]
    gathered = jnp.concatenate([audio_tokens.reshape(-1), speaker_of])[None]
    for move in (ACROSS_X, ONE_ALONG, TWO_ALONG):
        gathered = jnp.concatenate([gathered, send(gathered, move)], axis=0)
    whole_audio = (
        gathered[:, : SPK * tokens * audio_width]
        .reshape(-1, SPK, tokens, audio_width)
        .transpose(1, 0, 2, 3)
        .reshape(-1, audio_width)
    )
    audio_length = whole_audio.shape[0] // SPK
    speakers = gathered[:2, SPK * tokens * audio_width :].astype(jnp.int32)
    own_block = lambda weights: lax.dynamic_slice(weights, (0, x * block), (audio_width, block))
    key_rows = add_rows(whole_audio, own_block(w_key)).astype(jnp.bfloat16)
    value_rows = add_rows(whole_audio, own_block(w_value)).astype(jnp.bfloat16)

    speaker = speakers.reshape(-1, 1)
    attended = []
    for weights, order, first, last in (
        (gathered_weights, by_core, 0, GATHERED_HEADS),
        (hopped_weights, by_core ^ z, GATHERED_HEADS, heads_block),
    ):
        at = slice(first * HD, last * HD)
        kept, sent = query_product(
            jnp.concatenate([place, order]), video_rows, near, weights
        )
        attended.append(
            head_pieces(
                attend(
                    kept,
                    send(sent, ACROSS_X),
                    key_rows[:, at],
                    value_rows[:, at],
                    speaker,
                    audio_length,
                )
            )
        )

    result = None
    first = 0
    for heads in OUT_CHUNKS:
        size = heads * HD
        weights = along_z(w_output[:, first : first + size])
        kept, sent = out_product(planes ^ h, attended, weights)
        result = finish(kept, send(sent, ACROSS_X), first, w_output.shape[1], result)
        first += size
    return result


def solution(mesh):
    in_specs = (
        P("ctx", None),
        P("ctx", "head"),
        P("ctx", "head"),
        P(None, "ctx", None),
        P(None, "head"),
        P(None, "head"),
        P(None, "ctx"),
        P(None, "ctx"),
    )
    out_specs = P("ctx", "head")
    planes = mesh.shape["ctx"] == 8 and mesh.shape["head"] == 4
    shards = plane_shards if planes else plain_shards
    return jax.shard_map(shards, mesh=mesh, in_specs=in_specs, out_specs=out_specs, check_vma=False)
```

```python
import functools

import jax
import jax.numpy as jnp
from jax import lax
from jax.experimental import pallas as pl
from jax.experimental.pallas import tpu as pltpu
from jax.sharding import PartitionSpec as P

HD = 128
SPK = 2
AXES = ("ctx", "head")
GATHERED_HEADS = 3
OUT_CHUNKS = (8, 2)


def add_rows(left_rows, shard_piece):
    return jnp.dot(left_rows, shard_piece, preferred_element_type=jnp.float32)


def plain_shards(video_rows, w_query, w_output, audio_tokens, w_key, w_value, row_lists, row_counts):
    rows_dev = video_rows.shape[0]
    columns = w_query.shape[1]
    heads_dev = columns // HD
    queries = add_rows(video_rows, lax.all_gather(w_query, "ctx", axis=0, tiled=True)).astype(
        jnp.bfloat16
    )
    whole_audio = lax.all_gather(audio_tokens, "ctx", axis=1, tiled=True)
    key_rows = jnp.einsum(
        "sta,ad->std", whole_audio, w_key, preferred_element_type=jnp.float32
    ).astype(jnp.bfloat16)
    value_rows = jnp.einsum(
        "sta,ad->std", whole_audio, w_value, preferred_element_type=jnp.float32
    ).astype(jnp.bfloat16)
    audio_length = key_rows.shape[1]
    position = jnp.arange(rows_dev, dtype=jnp.int32)
    score_scale = 1.0 / HD**0.5
    summed = jnp.zeros((rows_dev, columns), jnp.float32)
    for speaker in range(SPK):
        target = row_lists[speaker]
        row_live = position < row_counts[speaker, 0]
        picked = queries[target].reshape(rows_dev, heads_dev, HD)
        key_block = key_rows[speaker].reshape(audio_length, heads_dev, HD)
        value_block = value_rows[speaker].reshape(audio_length, heads_dev, HD)
        scores = (
            jnp.einsum("rhd,khd->hrk", picked, key_block, preferred_element_type=jnp.float32)
            * score_scale
        )
        scores = scores - jnp.max(scores, axis=-1, keepdims=True)
        weights = jnp.exp(scores)
        weights = (weights / jnp.sum(weights, axis=-1, keepdims=True)).astype(jnp.bfloat16)
        blended = jnp.einsum(
            "hrk,khd->rhd", weights, value_block, preferred_element_type=jnp.float32
        ).astype(jnp.bfloat16)
        blended = blended.reshape(rows_dev, columns).astype(jnp.float32)
        blended = jnp.where(row_live[:, None], blended, jnp.zeros_like(blended))
        summed = summed.at[target].add(blended)
    attended = summed.astype(jnp.bfloat16)
    all_heads = lax.all_gather(attended, "head", axis=1, tiled=True)
    result = add_rows(all_heads, lax.all_gather(w_output, "ctx", axis=0, tiled=True))
    return result.astype(jnp.bfloat16)


def pairs(planes, move):
    found = []
    for z in range(planes):
        for x in range(2):
            for h in range(4):
                to = move(z, x, h)
                found.append(((2 * z + x) * 4 + h, (2 * to[0] + to[1]) * 4 + to[2]))
    return found


ACROSS_X = pairs(4, lambda z, x, h: (z, 1 - x, h))
ACROSS_Y = pairs(4, lambda z, x, h: (z, x, h ^ 2))
ACROSS_CORE = pairs(4, lambda z, x, h: (z, x, h ^ 1))
ONE_ALONG = pairs(4, lambda z, x, h: (z ^ 1, x, h))
TWO_ALONG = pairs(4, lambda z, x, h: (z ^ 2, x, h))
MID_TO_END = [pair for pair in ONE_ALONG if pair[0] // 8 in (1, 2)]
MID_TO_MID = pairs(4, lambda z, x, h: (3 - z if z in (1, 2) else z, x, h))
SAME_X = [[0, 2, 4, 6], [1, 3, 5, 7]]


def send(value, move):
    return lax.ppermute(value, AXES, move)


def along_z(value):
    return lax.all_gather(value, "ctx", axis=0, axis_index_groups=SAME_X)


def diagonal(groups):
    shape = (groups * 128, 128)
    row = lax.broadcasted_iota(jnp.int32, shape, 0) % 128
    return row == lax.broadcasted_iota(jnp.int32, shape, 1)


def pack(value, packed):
    rows, columns = value.shape
    groups = rows // 128
    peak = jnp.max(jnp.abs(value), axis=1, keepdims=True)
    power = jnp.clip(jnp.floor(jnp.log2(jnp.maximum(peak, 1e-33))) + 1.0, -110.0, 120.0)
    scaled = jnp.clip(jnp.round(value * jnp.exp2(15.0 - power)), -32767.0, 32767.0)
    packed[:rows, :] = scaled.astype(jnp.int32).astype(jnp.int16)
    spread = jnp.where(diagonal(groups), power, 0.0).reshape(groups, 128, 128).sum(axis=1)
    spread = jnp.concatenate([spread, jnp.zeros((16 - groups, 128), jnp.float32)], axis=0)
    packed[rows:, :128] = spread.astype(jnp.int32).astype(jnp.int16)
    packed[rows:, 128:] = jnp.zeros((16, columns - 128), jnp.int16)


def row_scale(packed):
    groups = (packed.shape[0] - 16) // 128
    spread = packed[groups * 128 :, :128].astype(jnp.int32).astype(jnp.float32)[:groups]
    spread = jnp.broadcast_to(spread[:, None, :], (groups, 128, 128)).reshape(groups * 128, 128)
    power = jnp.sum(jnp.where(diagonal(groups), spread, 0.0), axis=1, keepdims=True)
    return jnp.exp2(power - 15.0)


def unpack(packed, scale):
    return packed[: packed.shape[0] - 16, :].astype(jnp.int32).astype(jnp.float32) * scale


def query_body(place, *refs):
    own, near, (keep_weights, send_weights, kept, sent) = refs[:4], refs[4:8], refs[8:]

    def write(lefts):
        for weights, result in ((send_weights, sent), (keep_weights, kept)):
            total = None
            for j in range(4):
                term = jnp.dot(
                    lefts[j][...], weights[place[6 + j]], preferred_element_type=jnp.float32
                )
                total = term if total is None else total + term
            result[...] = total

    first_group = pl.program_id(0) < pl.num_programs(0) // 2
    pl.when(first_group)(lambda: write(own))
    pl.when(jnp.logical_not(first_group))(lambda: write(near))


def query_product(place, video_rows, near, weights):
    rows = video_rows.shape[0]
    depth, columns = weights.shape[1:]
    step = rows
    half = columns // 2
    own_specs = [
        pl.BlockSpec(
            (step, depth),
            functools.partial(lambda j, i, place: (0, place[j]), j),
        )
        for j in range(4)
    ]
    near_specs = [
        pl.BlockSpec(
            (step, depth), functools.partial(lambda j, i, place: (0, j % 2), j)
        )
        for j in range(4)
    ]
    part = jax.ShapeDtypeStruct((2 * rows, half), jnp.float32)
    return pl.pallas_call(
        query_body,
        grid_spec=pltpu.PrefetchScalarGridSpec(
            num_scalar_prefetch=1,
            grid=(2,),
            in_specs=own_specs
            + near_specs
            + [
                pl.BlockSpec((4, depth, half), lambda i, place: (0, 0, place[4])),
                pl.BlockSpec((4, depth, half), lambda i, place: (0, 0, place[5])),
            ],
            out_specs=[pl.BlockSpec((step, half), lambda i, place: (i, 0))] * 2,
        ),
        out_shape=[part, part],
        cost_estimate=pl.CostEstimate(
            flops=16 * rows * depth * columns,
            transcendentals=0,
            bytes_accessed=8 * (2 * rows + columns) * depth + 8 * rows * columns,
        ),
        name="query_product",
    )(place, *([video_rows] * 4), near[0], near[0], near[1], near[1], weights, weights)


def out_body(place, *refs, k_sizes):
    *lefts, weights, kept, sent = refs
    total = None
    for j in range(4):
        left = jnp.concatenate([lefts[i * 4 + j][...] for i in range(len(k_sizes))], axis=1)
        term = jnp.dot(left, weights[place[j]], preferred_element_type=jnp.float32)
        total = term if total is None else total + term
    pl.when(pl.program_id(0) == 0)(lambda: pack(total, sent))
    pl.when(pl.program_id(0) == 1)(lambda: kept.__setitem__(..., total))


def out_product(place, groups, weights):
    rows = groups[0][0].shape[0]
    k_sizes = tuple(group[0].shape[1] for group in groups)
    columns = weights.shape[2]
    step = rows // 2
    left_specs = [
        pl.BlockSpec(
            (step, size), functools.partial(lambda skip, i, place: (1 - i + skip, 0), skip)
        )
        for size in k_sizes
        for skip in (0, 0, 0, 2)
    ]
    lefts = [piece for own, core, over_y in groups for piece in (own, core, over_y, core)]
    return pl.pallas_call(
        functools.partial(out_body, k_sizes=k_sizes),
        grid_spec=pltpu.PrefetchScalarGridSpec(
            num_scalar_prefetch=1,
            grid=(2,),
            in_specs=left_specs + [pl.BlockSpec(weights.shape, lambda i, place: (0, 0, 0))],
            out_specs=[
                pl.BlockSpec((step, columns), lambda i, place: (0, 0)),
                pl.BlockSpec((step + 16, columns), lambda i, place: (0, 0)),
            ],
        ),
        out_shape=[
            jax.ShapeDtypeStruct((step, columns), jnp.float32),
            jax.ShapeDtypeStruct((step + 16, columns), jnp.int16),
        ],
        cost_estimate=pl.CostEstimate(
            flops=8 * rows * sum(k_sizes) * columns,
            transcendentals=0,
            bytes_accessed=8 * (rows + columns) * sum(k_sizes) + 4 * rows * columns,
        ),
        name="out_product",
    )(place, *lefts, weights)


def attend_body(kept, received, keys, values, speaker, attended, *, audio_length, heads):
    scale = 1.0 / HD**0.5
    of_row = speaker[...]
    lane = lax.broadcasted_iota(jnp.int32, (kept.shape[0], SPK * audio_length), 1)
    of_key = jnp.where(lane < audio_length, 1, 2)
    own_key = of_key == of_row
    live = of_row > 0
    for head in range(heads):
        at = slice(head * HD, (head + 1) * HD)
        query = (kept[:, at] + received[:, at]).astype(jnp.bfloat16)
        scores = (
            lax.dot_general(
                query, keys[:, at], (((1,), (1,)), ((), ())), preferred_element_type=jnp.float32
            )
            * scale
        )
        scores = jnp.where(own_key, scores, -1e30)
        scores = scores - jnp.max(scores, axis=-1, keepdims=True)
        weights = jnp.exp(scores)
        weights = (weights / jnp.sum(weights, axis=-1, keepdims=True)).astype(jnp.bfloat16)
        blended = jnp.dot(weights, values[:, at], preferred_element_type=jnp.float32)
        attended[:, at] = jnp.where(live, blended, 0.0).astype(jnp.bfloat16)


def attend(kept, received, keys, values, speaker, audio_length):
    rows, columns = kept.shape
    step = rows // 4
    at = lambda i: (i, 0)
    whole = pl.BlockSpec(keys.shape, lambda i: (0, 0))
    return pl.pallas_call(
        functools.partial(attend_body, audio_length=audio_length, heads=columns // HD),
        grid=(4,),
        in_specs=[
            pl.BlockSpec((step, columns), at),
            pl.BlockSpec((step, columns), lambda i: ((i + 2) % 4, 0)),
            whole,
            whole,
            pl.BlockSpec((step, 1), at),
        ],
        out_specs=pl.BlockSpec((step, columns), at),
        out_shape=jax.ShapeDtypeStruct((rows, columns), jnp.bfloat16),
        cost_estimate=pl.CostEstimate(
            flops=4 * rows * columns * SPK * audio_length,
            transcendentals=rows * SPK * audio_length * columns // HD,
            bytes_accessed=10 * rows * columns,
        ),
        name="attend",
    )(kept, received, keys, values, speaker)


def finish_body(kept, received, scales, *refs):
    refs[-1][...] = (kept[...] + unpack(received, row_scale(scales))).astype(
        jnp.bfloat16
    )


def finish(kept, received, first, whole, result):
    rows, columns = kept.shape
    width = 4 * HD if columns % (4 * HD) == 0 and first % (4 * HD) == 0 else 2 * HD
    at = lambda j: (0, j)
    given = [] if result is None else [result]
    return pl.pallas_call(
        finish_body,
        grid=(columns // width,),
        in_specs=[
            pl.BlockSpec((rows, width), at),
            pl.BlockSpec((rows + 16, width), at),
            pl.BlockSpec((rows + 16, 128), lambda j: (0, 0)),
        ]
        + [pl.BlockSpec(memory_space=pl.ANY)] * len(given),
        out_specs=pl.BlockSpec((rows, width), lambda j: (0, first // width + j)),
        out_shape=jax.ShapeDtypeStruct((rows, whole), jnp.bfloat16),
        input_output_aliases={3: 0} if given else {},
        cost_estimate=pl.CostEstimate(
            flops=2 * rows * columns, transcendentals=0, bytes_accessed=8 * rows * columns
        ),
        name="finish",
    )(kept, received, received, *given)


def head_pieces(value):
    over_y = send(value, ACROSS_Y)
    return value, send(jnp.concatenate([value, over_y], axis=0), ACROSS_CORE), over_y


def plane_shards(video_rows, w_query, w_output, audio_tokens, w_key, w_value, row_lists, row_counts):
    rows = video_rows.shape[0]
    block = w_query.shape[0]
    audio_width = audio_tokens.shape[2]
    ctx = lax.axis_index("ctx").astype(jnp.int32)
    h = lax.axis_index("head").astype(jnp.int32)
    x = ctx % 2
    core = h % 2

    z = ctx // 2
    is_mid = (z == 1) | (z == 2)

    def of_blocks(value, first, last):
        first, last = first * HD, last * HD
        return jnp.concatenate(
            [value[:, first:last], value[:, block + first : block + last]], axis=1
        )

    heads_block = block // HD
    gathered_weights = along_z(of_blocks(w_query, 0, GATHERED_HEADS))
    piece = of_blocks(w_query, GATHERED_HEADS, heads_block)
    swapped = send(piece, ONE_ALONG)
    opposite = send(piece, MID_TO_MID)
    last = send(swapped, MID_TO_MID)
    to_end = send(opposite, MID_TO_END)
    last_to_end = send(last, MID_TO_END)
    hopped_weights = jnp.stack(
        [
            piece,
            swapped,
            jnp.where(is_mid, last, to_end),
            jnp.where(is_mid, opposite, last_to_end),
        ]
    )

    near_block = lambda plane: lax.dynamic_slice(
        video_rows, (0, (2 * plane + 1 - x) * block), (rows, block)
    )
    near_half = jnp.concatenate([near_block(2 * core), near_block(2 * core + 1)], axis=1)
    near_half, piece = lax.optimization_barrier((near_half, piece))
    near_half = send(near_half, ACROSS_X)
    near = [near_half, send(near_half, ACROSS_CORE)]
    planes = jnp.arange(4, dtype=jnp.int32)
    by_core = planes ^ (2 * core)
    place = jnp.concatenate([2 * by_core + x, jnp.stack([x, 1 - x])])

    position = jnp.arange(rows, dtype=jnp.int32)
    named = (row_lists[:, :, None] == position[None, None, :]) & (
        position[None, :, None] < row_counts[:, :, None]
    )
    speaker_of = jnp.sum(
        jnp.any(named, axis=1) * jnp.array([[1], [2]], jnp.int32), axis=0
    ).astype(jnp.bfloat16)
    tokens = audio_tokens.shape[1]
    gathered = jnp.concatenate([audio_tokens.reshape(-1), speaker_of])[None]
    for move in (ACROSS_X, ONE_ALONG, TWO_ALONG):
        gathered = jnp.concatenate([gathered, send(gathered, move)], axis=0)
    whole_audio = (
        gathered[:, : SPK * tokens * audio_width]
        .reshape(-1, SPK, tokens, audio_width)
        .transpose(1, 0, 2, 3)
        .reshape(-1, audio_width)
    )
    audio_length = whole_audio.shape[0] // SPK
    speakers = gathered[:2, SPK * tokens * audio_width :].astype(jnp.int32)
    own_block = lambda weights: lax.dynamic_slice(weights, (0, x * block), (audio_width, block))
    key_rows = add_rows(whole_audio, own_block(w_key)).astype(jnp.bfloat16)
    value_rows = add_rows(whole_audio, own_block(w_value)).astype(jnp.bfloat16)

    speaker = speakers.reshape(-1, 1)
    attended = []
    for weights, order, first, last in (
        (gathered_weights, by_core, 0, GATHERED_HEADS),
        (hopped_weights, by_core ^ z, GATHERED_HEADS, heads_block),
    ):
        at = slice(first * HD, last * HD)
        kept, sent = query_product(
            jnp.concatenate([place, order]), video_rows, near, weights
        )
        attended.append(
            head_pieces(
                attend(
                    kept,
                    send(sent, ACROSS_X),
                    key_rows[:, at],
                    value_rows[:, at],
                    speaker,
                    audio_length,
                )
            )
        )

    result = None
    first = 0
    for heads in OUT_CHUNKS:
        size = heads * HD
        weights = along_z(w_output[:, first : first + size])
        kept, sent = out_product(planes ^ h, attended, weights)
        result = finish(kept, send(sent, ACROSS_X), first, w_output.shape[1], result)
        first += size
    return result


def solution(mesh):
    in_specs = (
        P("ctx", None),
        P("ctx", "head"),
        P("ctx", "head"),
        P(None, "ctx", None),
        P(None, "head"),
        P(None, "head"),
        P(None, "ctx"),
        P(None, "ctx"),
    )
    out_specs = P("ctx", "head")
    planes = mesh.shape["ctx"] == 8 and mesh.shape["head"] == 4
    shards = plane_shards if planes else plain_shards
    return jax.shard_map(shards, mesh=mesh, in_specs=in_specs, out_specs=out_specs, check_vma=False)
```
